256 devices in a mesh: dp: 4 (over z_lo), ctx: 64 (over z_hi, x, y, core).
Axes of the slice: x: 4, y: 4, z: 8 (z_hi: 2, z_lo: 4; z = z_hi * 4 + z_lo), core: 2. Of those that a mesh axis runs over, the one named last changes fastest.
Arguments:
- inputs: bfloat16 [4, 131072, 256], P('dp', 'ctx'), may hold values from -16 to 16
- grad_out: bfloat16 [4, 131072, 256], P('dp', 'ctx'), may hold values from -6 to 6
- w_in: bfloat16 [256, 768], replicated, may hold values from -0.375 to 0.375
- filter_real: float32 [512, 512, 16], P('ctx'), may hold values from -12 to 12, as said below
- filter_imag: float32 [512, 512, 16], P('ctx'), may hold values from -12 to 12, as said below
Outputs:
- gated_out: bfloat16 [4, 131072, 256], P('dp', 'ctx')
- grad_w_in: float32 [256, 768], P('dp')
The draws below stay inside these ranges and needn't reach their ends.
Inputs may be any that keep to these rules, and one draw needn't show every extreme that they name: Each long filter is real: with P = 262144, filter_real at frequency (P - f) mod P equals filter_real at frequency f. Each long filter is real: with P = 262144, filter_imag at frequency (P - f) mod P is minus filter_imag at frequency f.
All inputs are finite; a program needn't handle non-finite values.
Results may differ from the reference program's by a relative error of at most 0.011.
Values may be sent and summed in bfloat16 or wider, within the bound.
A program may use at most 128 MiB of HBM per device.

```python
import math
import jax
import jax.numpy as jnp
from jax import lax

C = 256
N1 = 512
N2 = 512
FG = 16
BATCH = 4
SEQ = 131072


def spectrum_pair(key):
    base_key = jax.random.fold_in(key, 31)
    real_key, imag_key = jax.random.split(base_key, 2)
    shape_three = (N1, N2, FG)
    real_noise = jax.random.truncated_normal(real_key, -4.0, 4.0, shape_three, jnp.float32)
    imag_noise = jax.random.truncated_normal(imag_key, -4.0, 4.0, shape_three, jnp.float32)
    row_index = jnp.arange(N1, dtype=jnp.int32)
    col_index = jnp.arange(N2, dtype=jnp.int32)
    mirror_row = (N1 - row_index) % N1
    mirror_col = (N2 - col_index[None, :] - (row_index[:, None] > 0).astype(jnp.int32)) % N2
    mirror_real = real_noise[mirror_row[:, None], mirror_col]
    mirror_imag = imag_noise[mirror_row[:, None], mirror_col]
    half_root = math.sqrt(0.5)
    spec_real = (real_noise + mirror_real) * half_root
    spec_imag = (imag_noise - mirror_imag) * half_root
    return (spec_real.astype(jnp.float32), spec_imag.astype(jnp.float32))


def draw_filter_real(key, part):
    return spectrum_pair(key)[0]


def draw_filter_imag(key, part):
    return spectrum_pair(key)[1]


def raised(values, rng, source, target, shards_of, factor):
    owner, partner = [(jnp.arange(values.shape[axis_at]) // (values.shape[axis_at] // shards_of)).reshape([-1 if axis == axis_at else 1 for axis in range(values.ndim)]) for axis_at in (source, target)]
    chosen = jax.random.permutation(rng, shards_of)[partner]
    strong = (owner == chosen) | (owner == (partner + shards_of // 2) % shards_of)
    return jnp.where(strong, factor * values, values)


def block_levels(stream_key, shape, shards, smallest, largest):
    gain, own = 1.0, jax.random.fold_in(stream_key, 6)
    for position, parts in shards:
        draws = jnp.exp(jax.random.uniform(jax.random.fold_in(own, position), (parts,), jnp.float32, smallest / len(shards), largest / len(shards)))
        gain = gain * jnp.repeat(draws, shape[position] // parts).reshape([-1 if axis == position else 1 for axis in range(len(shape))])
    return gain


def bell_draw(stream_key, extent, deviation, most, pieces=(), kind=jnp.bfloat16):
    factor_of = block_levels(stream_key, extent, pieces, -0.22, 0.18) if pieces else 1.0
    values = jax.random.normal(stream_key, extent, jnp.float32) * deviation * factor_of
    return jnp.minimum(jnp.maximum(values, -most), most).astype(kind)


def bell_draw_with(stream_key, extent, scale, bound, cuts, heavy, kind=jnp.bfloat16):
    entries = scale * jax.random.normal(stream_key, extent, jnp.float32)
    if cuts:
        entries = entries * block_levels(stream_key, extent, cuts, -0.22, 0.18)
    return jnp.clip(raised(entries, jax.random.fold_in(stream_key, 3), *heavy), -bound, bound).astype(kind)


def setup_inputs(seed: int = 0) -> dict:
    arg_keys = jax.random.split(jax.random.key(seed), 6)
    return {
        "inputs": bell_draw_with(arg_keys[0], (BATCH, SEQ, C), 1.0, 16.0, ((0, 4), (1, 64)), (1, 2, 64, 4.0)),
        "grad_out": bell_draw(arg_keys[1], (BATCH, SEQ, C), 1.0, 6.0, ((0, 4), (1, 64))),
        "w_in": bell_draw(arg_keys[2], (C, 3 * C), C ** -0.5, 0.375),
        "filter_real": draw_filter_real(jax.random.fold_in(arg_keys[5], 71), 0),
        "filter_imag": draw_filter_imag(jax.random.fold_in(arg_keys[5], 71), 0),
    }


def widen(array_value):
    return lax.optimization_barrier(array_value).astype(jnp.float32)

def dft_tables(row_index, col_index, period, factor):
    phase_angle = (row_index[:, None] * col_index[None, :] % period).astype(jnp.float32) * (2.0 * math.pi / period)
    return ((jnp.cos(phase_angle) * factor).astype(jnp.bfloat16), (jnp.sin(phase_angle) * factor).astype(jnp.bfloat16))

def twiddle_tables(row_index, col_index, period):
    phase_angle = (row_index[:, None] * col_index[None, :] % period).astype(jnp.float32) * (2.0 * math.pi / period)
    return (jnp.cos(phase_angle)[:, :, None], jnp.sin(phase_angle)[:, :, None])

def combine(cos_part, sin_part, orient):
    real_part = cos_part[:, :, 0] - orient * sin_part[:, :, 1]
    imag_part = cos_part[:, :, 1] + orient * sin_part[:, :, 0]
    return (real_part, imag_part)

def rotate(real_part, imag_part, cos_table, sin_table, orient):
    new_real = real_part * cos_table - orient * imag_part * sin_table
    new_imag = imag_part * cos_table + orient * real_part * sin_table
    return (new_real, new_imag)

def pack_complex(real_part, imag_part):
    return jnp.stack([real_part, imag_part], axis=2).astype(jnp.bfloat16)

def long_conv(block_data, tables, filter_real, filter_imag):
    cos_one, sin_one, cos_two, sin_two, twist_cos, twist_sin = tables
    half_rows = cos_one.shape[1]
    shaped = widen(block_data).reshape(half_rows, cos_two.shape[0], 2, block_data.shape[-1])
    cos_part = jnp.einsum('ft,tcpm->fcpm', cos_one, shaped)
    sin_part = jnp.einsum('ft,tcpm->fcpm', sin_one, shaped)
    real_part, imag_part = combine(cos_part, sin_part, -1.0)
    real_part, imag_part = rotate(real_part, imag_part, twist_cos, twist_sin, -1.0)
    columns = widen(pack_complex(real_part, imag_part))
    cos_part = jnp.einsum('fcpm,cg->fgpm', columns, cos_two)
    sin_part = jnp.einsum('fcpm,cg->fgpm', columns, sin_two)
    real_part, imag_part = combine(cos_part, sin_part, -1.0)
    prod_real = real_part * filter_real - imag_part * filter_imag
    prod_imag = real_part * filter_imag + imag_part * filter_real
    product = widen(pack_complex(prod_real, prod_imag))
    cos_part = jnp.einsum('fgpm,gc->fcpm', product, cos_two)
    sin_part = jnp.einsum('fgpm,gc->fcpm', product, sin_two)
    real_part, imag_part = combine(cos_part, sin_part, 1.0)
    real_part, imag_part = rotate(real_part, imag_part, twist_cos, twist_sin, 1.0)
    returned = widen(pack_complex(real_part, imag_part))
    cos_part = jnp.einsum('ft,fcpm->tcpm', cos_one, returned)
    sin_part = jnp.einsum('ft,fcpm->tcpm', sin_one, returned)
    real_part, imag_part = combine(cos_part, sin_part, 1.0)
    return pack_complex(real_part, imag_part).reshape(block_data.shape)

def reference(inputs, grad_out, w_in, filter_real, filter_imag):
    seq_count, seq_len, chan_total = inputs.shape
    chan_half = chan_total // 2
    period = N1 * N2
    full_index = jnp.arange(N1, dtype=jnp.int32)
    half_index = jnp.arange(N1 // 2, dtype=jnp.int32)
    second_index = jnp.arange(N2, dtype=jnp.int32)
    cos_one, sin_one = dft_tables(full_index, half_index, N1, 1.0 / math.sqrt(N1))
    cos_two, sin_two = dft_tables(second_index, second_index, N2, 1.0 / math.sqrt(N2))
    twist_cos, twist_sin = twiddle_tables(full_index, second_index, period)
    tables = (widen(cos_one), widen(sin_one), widen(cos_two), widen(sin_two), twist_cos, twist_sin)
    filter_count = filter_real.shape[2]

    def conv_all(signal, orient):
        blocks = signal.reshape(seq_len, 2, chan_half // filter_count, filter_count).transpose(2, 0, 1, 3)

        def one_block(block_data):
            return long_conv(block_data, tables, filter_real, orient * filter_imag)
        result = lax.map(one_block, blocks)
        return result.transpose(1, 2, 0, 3).reshape(seq_len, chan_total)
    weight_total = jnp.zeros((chan_total, 3 * chan_total), jnp.float32)
    gated_list = []
    for seq_index in range(seq_count):
        tokens = inputs[seq_index]
        cotangent = widen(grad_out[seq_index])
        features = jnp.dot(widen(tokens), widen(w_in)).astype(jnp.bfloat16)
        wide_features = widen(features)
        gate_part = wide_features[:, :chan_total]
        key_part = wide_features[:, chan_total:2 * chan_total]
        value_part = wide_features[:, 2 * chan_total:]
        mixed = (key_part * value_part).astype(jnp.bfloat16)
        smooth = widen(conv_all(mixed, 1.0))
        gated_list.append((gate_part * smooth).astype(jnp.bfloat16))
        grad_smooth = (cotangent * gate_part).astype(jnp.bfloat16)
        grad_gate = (cotangent * smooth).astype(jnp.bfloat16)
        grad_mixed = widen(conv_all(grad_smooth, -1.0))
        grad_key = (grad_mixed * value_part).astype(jnp.bfloat16)
        grad_value = (grad_mixed * key_part).astype(jnp.bfloat16)
        grad_features = jnp.concatenate([grad_gate, grad_key, grad_value], axis=1)
        weight_total = weight_total + lax.dot_general(widen(tokens), widen(grad_features), (((0,), (0,)), ((), ())))
    grad_w_in = weight_total * (1.0 / math.sqrt(seq_count * seq_len))
    return (jnp.stack(gated_list, axis=0), grad_w_in)
```

```python
import math

import jax
import jax.numpy as jnp
import numpy as np
from jax import lax
from jax.experimental import pallas as pl
from jax.experimental.pallas import tpu as pltpu
from jax.sharding import PartitionSpec as P

N1 = 512
N2 = 512
ROWS = 272
NCH = 2
MESH = pl.DeviceIdType.MESH
BF = jnp.bfloat16
F32 = jnp.float32


def tables():
    half = N1 // 2
    period = N1 * N2
    t1 = np.arange(half)
    fwd = np.zeros((2, 2 * ROWS, half), np.float64)
    inv = np.zeros((2, half, 2 * ROWS), np.float64)
    base = np.zeros((2, ROWS // 8), np.int64)
    for zh in range(2):
        rows = np.concatenate(
            [zh * half + np.arange(half), (1 - zh) * half + np.arange(8), np.zeros(8, np.int64)]
        )
        base[zh] = rows[::8]
        angle = 2.0 * np.pi * ((rows[:, None] * t1[None, :]) % N1) / N1
        scale = 1.0 / math.sqrt(N1)
        cos = (np.cos(angle) * scale).astype(BF).astype(np.float64)
        sin = (np.sin(angle) * scale).astype(BF).astype(np.float64)
        cos[half + 8 :] = 0.0
        sin[half + 8 :] = 0.0
        fwd[zh, :ROWS] = cos
        fwd[zh, ROWS:] = -sin
        weight = np.where((rows == 0) | (rows == half), 1.0, 2.0)
        weight[half + 1 :] = 0.0
        inv[zh, :, :ROWS] = (weight[:, None] * cos).T
        inv[zh, :, ROWS:] = -(weight[:, None] * sin).T
    t2 = np.arange(N2)
    angle = 2.0 * np.pi * ((t2[:, None] * t2[None, :]) % N2) / N2
    cos2 = np.cos(angle) / math.sqrt(N2)
    sin2 = np.sin(angle) / math.sqrt(N2)
    two = np.stack([cos2, sin2, -sin2])
    coarse = 2.0 * np.pi * ((base[:, :, None] * t2) % period) / period
    fine = 2.0 * np.pi * ((np.arange(8)[:, None] * t2) % period) / period
    coarse = np.stack([np.cos(coarse), np.sin(coarse)], axis=1)[:, :, :, None, :]
    fine = np.stack([np.cos(fine), np.sin(fine)])
    order = np.arange(128)
    zh, g, i4 = order // 64, (order // 4) % 16, order % 4
    perm = np.zeros((128, 128))
    perm[order, zh * 64 + i4 * 16 + g] = 1.0
    return (
        fwd.astype(BF),
        inv.astype(BF),
        two.astype(BF),
        coarse.astype(np.float32),
        fine.astype(np.float32),
        perm.astype(BF),
        perm.T.copy().astype(BF),
        np.eye(256).astype(BF),
    )


def nt(a, b):
    return lax.dot_general(a, b, (((1,), (1,)), ((), ())), preferred_element_type=F32)


def nn(a, b):
    return jnp.dot(a, b, preferred_element_type=F32)


def mingle(a, b):
    low = lax.broadcasted_iota(jnp.int32, a.shape, 1) < 4
    first = jnp.where(low, a, pltpu.roll(b, 4, 1))
    second = jnp.where(low, pltpu.roll(a, 4, 1), b)
    return first, second


def kernel(
    x_ref, g_ref, w_ref, fr_in, fi_in, fwd_any, inv_any, two_any, coarse_ref, fine_ref,
    perm_ref, permt_ref, eye_ref,
    out_ref, grad_ref,
    fwd, inv, tab2, tab3, xt, wt, feat, gt, fsc, fsend, frecv, fre, fim, twc, tws,
    send_in, recv_in, mix, spec, prod, ret, send_out, recv_out,
    part, precv, zsend, zrecv, fin, frows,
    tab_sem, fsem_s, fsem_r, in_s, in_r, out_s, out_r, p_s, p_r, z_s, z_r, g_s, g_r,
):
    zl = lax.axis_index("dp")
    ctx = lax.axis_index("ctx")
    core = ctx % 2
    s = ctx % 32
    zh = ctx // 32
    chip = s // 2

    def ctx_peer(o):
        oc, oy, ox, oz = o % 2, (o // 2) % 4, (o // 8) % 4, o // 32
        cy, cx = (ctx // 2) % 4, (ctx // 8) % 4
        return ((((zh + oz) % 2) * 4 + (cx + ox) % 4) * 4 + (cy + oy) % 4) * 2 + (core + oc) % 2

    barrier = pltpu.get_barrier_semaphore()

    def greet(o, carry):
        pl.semaphore_signal(barrier, inc=1, device_id={"ctx": ctx_peer(o)}, device_id_type=MESH)
        return carry

    lax.fori_loop(1, 64, greet, 0)

    def greet_z(o, carry):
        pl.semaphore_signal(
            barrier,
            inc=1,
            device_id={"dp": (zl + 1 + o // 2) % 4, "ctx": (o % 2) * 32 + s},
            device_id_type=MESH,
        )
        return carry

    lax.fori_loop(0, 6, greet_z, 0)

    loads = [
        pltpu.make_async_copy(fwd_any.at[zh], fwd, tab_sem.at[0]),
        pltpu.make_async_copy(inv_any.at[zh], inv, tab_sem.at[1]),
        pltpu.make_async_copy(two_any.at[0], tab2.at[0:512, 0:512], tab_sem.at[2]),
        pltpu.make_async_copy(two_any.at[0], tab2.at[512:1024, 512:1024], tab_sem.at[3]),
        pltpu.make_async_copy(two_any.at[1], tab2.at[512:1024, 0:512], tab_sem.at[4]),
        pltpu.make_async_copy(two_any.at[2], tab2.at[0:512, 512:1024], tab_sem.at[5]),
        pltpu.make_async_copy(two_any.at[0], tab3.at[0:512, 0:512], tab_sem.at[6]),
        pltpu.make_async_copy(two_any.at[0], tab3.at[512:1024, 512:1024], tab_sem.at[7]),
        pltpu.make_async_copy(two_any.at[1], tab3.at[0:512, 512:1024], tab_sem.at[8]),
        pltpu.make_async_copy(two_any.at[2], tab3.at[512:1024, 0:512], tab_sem.at[9]),
    ]
    for load in loads:
        load.start()

    for h in range(NCH):
        for p in range(3):
            cols = w_ref[:, p * 256 + h * 128 : p * 256 + (h + 1) * 128]
            wt[h, p * 128 : (p + 1) * 128, :] = nt(perm_ref[...], cols).astype(BF)

    def project(h):
        for jj in range(2):
            mixed, smoothed = [], []
            for j in (2 * jj, 2 * jj + 1):
                xs = x_ref[j * 512 : (j + 1) * 512, :]
                rows = nt(wt[h], xs).astype(BF)
                feat[h, j] = rows
                rows = rows.astype(F32)
                mixed.append((rows[128:256] * rows[256:384]).reshape(16, 8, 512))
                gs = nt(perm_ref[...], g_ref[j * 512 : (j + 1) * 512, h * 128 : (h + 1) * 128])
                gt[h, j] = gs.astype(BF)
                smoothed.append((gs * rows[0:128]).reshape(16, 8, 512))
            for kind, pair in enumerate((mixed, smoothed)):
                even, odd = mingle(pair[0], pair[1])
                mix[kind, :, 0, jj * 8 : jj * 8 + 8, :] = even
                mix[kind, :, 1, jj * 8 : jj * 8 + 8, :] = odd
        for kind in range(2):
            block = mix[kind].reshape(32, 16, 512).astype(BF)
            send_in[h, :, kind] = block

    def offset(k):
        return (k + 31) % 63 + 1

    def in_copy(h, k):
        peer = ctx_peer(offset(k))
        return pltpu.make_async_remote_copy(
            send_in.at[h, peer // 2, peer % 2],
            recv_in.at[h, ctx],
            in_s.at[h],
            in_r.at[h],
            device_id={"ctx": peer},
            device_id_type=MESH,
        )

    def send_chunk(h):
        def step(k, carry):
            in_copy(h, k).start()
            return carry

        lax.fori_loop(0, 63, step, 0)
        recv_in[h, ctx] = send_in[h, ctx // 2, ctx % 2]

    def filter_copy(o):
        peer = zh * 32 + ctx_peer(o) % 32
        return pltpu.make_async_remote_copy(
            fsend.at[(peer // 2) % 16],
            frecv.at[s],
            fsem_s,
            fsem_r,
            device_id={"ctx": peer},
            device_id_type=MESH,
        )

    def extra_copy(o):
        peer = (1 - zh) * 32 + o
        return pltpu.make_async_remote_copy(
            fsend.at[(peer // 2) % 16],
            frecv.at[32],
            fsem_s,
            fsem_r,
            device_id={"ctx": peer},
            device_id_type=MESH,
        )

    project(0)
    pl.semaphore_wait(barrier, 69)
    send_chunk(0)

    for which, ref in enumerate((fr_in, fi_in)):
        turned = nt(eye_ref[0:16, 0:16], ref[...].astype(BF))
        for k in range(8):
            for q in range(4):
                fsc[q, pl.ds(which * 8 + k, 16, stride=16), :] = turned[
                    :, k * 512 + q * 128 : k * 512 + (q + 1) * 128
                ]
    for q in range(4):
        fsend[:, :, q * 128 : (q + 1) * 128] = fsc[q].reshape(16, 16, 128).astype(BF)

    def fstep(o, carry):
        filter_copy(o).start()
        return carry

    lax.fori_loop(1, 32, fstep, 0)
    frecv[s] = fsend[chip]

    @pl.when(s == 0)
    def _():
        def estep(o, carry):
            extra_copy(o).start()
            return carry

        lax.fori_loop(0, 32, estep, 0)

    frecv[33] = jnp.zeros((16, 512), BF)

    project(1)
    send_chunk(1)

    for j in range(4):
        xt[j] = nt(eye_ref[...], x_ref[j * 512 : (j + 1) * 512, :]).astype(BF)
    ca, sa = coarse_ref[zh, 0], coarse_ref[zh, 1]
    cb, sb = fine_ref[0][None], fine_ref[1][None]
    twc[...] = (ca * cb - sa * sb).reshape(ROWS, 512)
    tws[...] = (sa * cb + ca * sb).reshape(ROWS, 512)
    for load in loads:
        load.wait()
    pltpu.make_async_copy(frecv.at[pl.ds(0, 32)], frecv.at[pl.ds(0, 32)], fsem_r).wait()
    both = frecv[...].astype(F32)
    sign = (1 - 2 * core).astype(F32)
    fre[...] = both[:, 0:8].reshape(ROWS, 512)
    fim[...] = both[:, 8:16].reshape(ROWS, 512) * sign

    def out_copy(h, k):
        peer = ctx_peer(offset(k))
        return pltpu.make_async_remote_copy(
            send_out.at[h, peer],
            recv_out.at[h, ctx // 4, (ctx // 2) % 2, core],
            out_s.at[h],
            out_r.at[h],
            device_id={"ctx": peer},
            device_id_type=MESH,
        )

    def conv(h, carry):
        pltpu.make_async_copy(
            recv_in.at[h, pl.ds(0, 63)], recv_in.at[h, pl.ds(0, 63)], in_r.at[h]
        ).wait()
        for q in range(4):
            lanes = slice(q * 128, (q + 1) * 128)
            spec[q] = recv_in[h, :, :, lanes].astype(F32).reshape(1024, 128)
        for i in range(4):
            sig = jnp.concatenate(
                [spec[q, pl.ds(i, 256, stride=4), :] for q in range(4)], axis=1
            ).astype(BF)
            one = nn(fwd[...], sig)
            re, im = one[:ROWS], one[ROWS:]
            c, sn = twc[...], tws[...]
            prod[:, 0:512] = (re * c + im * sn).astype(BF)
            prod[:, 512:1024] = (im * c - re * sn).astype(BF)
            two = nn(prod[...], tab2[...])
            dr, di = two[:, 0:512], two[:, 512:1024]
            a, b = fre[...], fim[...]
            prod[:, 0:512] = (dr * a - di * b).astype(BF)
            prod[:, 512:1024] = (dr * b + di * a).astype(BF)
            three = nn(prod[...], tab3[...])
            er, ei = three[:, 0:512], three[:, 512:1024]
            c, sn = twc[...], tws[...]
            ret[0:ROWS, :] = (er * c - ei * sn).astype(BF)
            ret[ROWS:, :] = (ei * c + er * sn).astype(BF)
            four = nn(inv[...], ret[...])
            for q in range(4):
                spec[q, pl.ds(i, 256, stride=4), :] = four[:, q * 128 : (q + 1) * 128]
        for q in range(4):
            lanes = slice(q * 128, (q + 1) * 128)
            send_out[h, :, :, lanes] = spec[q].reshape(64, 16, 128).astype(BF)

        def step(k, inner):
            out_copy(h, k).start()
            return inner

        lax.fori_loop(0, 63, step, 0)
        recv_out[h, ctx // 4, (ctx // 2) % 2, core] = send_out[h, ctx]
        return carry

    lax.fori_loop(0, NCH, conv, 0)

    def part_copy(h, o):
        peer = zh * 32 + ctx_peer(o) % 32
        return pltpu.make_async_remote_copy(
            part.at[h, peer % 32],
            precv.at[h, s],
            p_s.at[h],
            p_r.at[h],
            device_id={"ctx": peer},
            device_id_type=MESH,
        )

    def finish(h, carry):
        pltpu.make_async_copy(
            send_out.at[h, pl.ds(0, 63)], send_out.at[h, pl.ds(0, 63)], out_r.at[h]
        ).wait()
        total = jnp.zeros((256, 384), F32)
        lanes = pl.ds(pl.multiple_of(h * 128, 128), 128)
        for jj in range(2):
            got = []
            for kind in range(2):
                even = recv_out[h, :, 0, kind].astype(F32)[:, jj * 8 : jj * 8 + 8]
                odd = recv_out[h, :, 1, kind].astype(F32)[:, jj * 8 : jj * 8 + 8]
                first, second = mingle(even, odd)
                got.append((first.reshape(128, 512), second.reshape(128, 512)))
            for q in range(2):
                j = 2 * jj + q
                smooth, mixed = got[0][q], got[1][q]
                rows = feat[h, j].astype(F32)
                gate, key, value = rows[0:128], rows[128:256], rows[256:384]
                gated = nn(permt_ref[...], (gate * smooth).astype(BF))
                out_ref[j * 512 : (j + 1) * 512, lanes] = gated.T.astype(BF)
                grads = []
                for term in (gt[h, j].astype(F32) * smooth, mixed * value, mixed * key):
                    grads.append(nn(permt_ref[...], term.astype(BF)).astype(BF))
                total = total + nt(xt[j], jnp.concatenate(grads, axis=0))
        part[h] = total.reshape(32, 8, 384)

        def step(o, inner):
            part_copy(h, o).start()
            return inner

        lax.fori_loop(1, 32, step, 0)
        precv[h, s] = part[h, s]
        return carry

    lax.fori_loop(0, NCH, finish, 0)

    for h in range(NCH):
        pltpu.make_async_copy(
            part.at[h, pl.ds(0, 31)], part.at[h, pl.ds(0, 31)], p_r.at[h]
        ).wait()
        zsend[:, h * 384 : (h + 1) * 384] = jnp.sum(precv[h], axis=0)

    owner = s // 8
    here = zh * 4 + zl

    def z_copy(half):
        return pltpu.make_async_remote_copy(
            zsend,
            zrecv.at[here],
            z_s.at[half],
            z_r,
            device_id={"dp": owner, "ctx": half * 32 + s},
            device_id_type=MESH,
        )

    for half in range(2):
        mine = (zl == owner) & (zh == half)

        @pl.when(mine)
        def _():
            zrecv[here] = zsend[...]

        @pl.when(jnp.logical_not(mine))
        def _():
            z_copy(half).start()

    def g_copy(o):
        peer = zh * 32 + ctx_peer(o) % 32
        return pltpu.make_async_remote_copy(
            fin,
            frows.at[s % 8],
            g_s,
            g_r,
            device_id={"ctx": peer},
            device_id_type=MESH,
        )

    @pl.when(zl == owner)
    def _():
        pltpu.make_async_copy(zrecv.at[pl.ds(0, 7)], zrecv.at[pl.ds(0, 7)], z_r).wait()
        fin[...] = jnp.sum(zrecv[...], axis=0) * (1.0 / math.sqrt(524288.0))

        def step(o, inner):
            g_copy(o).start()
            return inner

        lax.fori_loop(1, 32, step, 0)
        frows[s % 8] = fin[...]
        pltpu.make_async_copy(frows.at[pl.ds(0, 7)], frows.at[pl.ds(0, 7)], g_r).wait()

    @pl.when(zl != owner)
    def _():
        pltpu.make_async_copy(frows, frows, g_r).wait()

    done = frows[...].reshape(64, 768)
    for h in range(NCH):
        for p in range(3):
            grad_ref[:, p * 256 + h * 128 : p * 256 + (h + 1) * 128] = done[
                :, h * 384 + p * 128 : h * 384 + (p + 1) * 128
            ]

    for h in range(NCH):
        for buf, sem in ((recv_in, in_s), (send_out, out_s)):
            pltpu.make_async_copy(
                buf.at[h, pl.ds(0, 63)], buf.at[h, pl.ds(0, 63)], sem.at[h]
            ).wait()
        pltpu.make_async_copy(
            part.at[h, pl.ds(0, 31)], part.at[h, pl.ds(0, 31)], p_s.at[h]
        ).wait()

    pltpu.make_async_copy(frecv.at[pl.ds(0, 31)], frecv.at[pl.ds(0, 31)], fsem_s).wait()

    @pl.when(s == 0)
    def _():
        pltpu.make_async_copy(frecv.at[pl.ds(0, 32)], frecv.at[pl.ds(0, 32)], fsem_s).wait()

    for half in range(2):
        @pl.when(jnp.logical_not((zl == owner) & (zh == half)))
        def _():
            z_copy(half).wait_send()

    @pl.when(zl == owner)
    def _():
        pltpu.make_async_copy(precv.at[0, pl.ds(0, 31)], precv.at[0, pl.ds(0, 31)], g_s).wait()
        pltpu.make_async_copy(precv.at[0, pl.ds(0, 31)], precv.at[0, pl.ds(0, 31)], g_s).wait()


def per_device(inputs, grad_out, w_in, filter_real, filter_imag):
    consts = [jnp.asarray(t) for t in tables()]
    vm = pl.BlockSpec(memory_space=pltpu.VMEM)
    anyspace = pl.BlockSpec(memory_space=pl.ANY)
    v = pltpu.VMEM
    dma = pltpu.SemaphoreType.DMA
    gated, grad = pl.pallas_call(
        kernel,
        out_shape=(
            jax.ShapeDtypeStruct((2048, 256), BF),
            jax.ShapeDtypeStruct((64, 768), F32),
        ),
        in_specs=[vm] * 5 + [anyspace] * 3 + [vm] * 5,
        out_specs=(vm, vm),
        scratch_shapes=[
            v((2 * ROWS, 256), BF),
            v((256, 2 * ROWS), BF),
            v((1024, 1024), BF),
            v((1024, 1024), BF),
            v((4, 256, 512), BF),
            v((NCH, 384, 256), BF),
            v((NCH, 4, 384, 512), BF),
            v((NCH, 4, 128, 512), BF),
            v((4, 256, 128), F32),
            v((16, 16, 512), BF),
            v((34, 16, 512), BF),
            v((ROWS, 512), F32),
            v((ROWS, 512), F32),
            v((ROWS, 512), F32),
            v((ROWS, 512), F32),
            v((NCH, 32, 2, 16, 512), BF),
            v((NCH, 64, 16, 512), BF),
            v((2, 16, 2, 16, 512), F32),
            v((4, 1024, 128), F32),
            v((ROWS, 1024), BF),
            v((2 * ROWS, 512), BF),
            v((NCH, 64, 16, 512), BF),
            v((NCH, 16, 2, 2, 16, 512), BF),
            v((NCH, 32, 8, 384), F32),
            v((NCH, 32, 8, 384), F32),
            v((8, 768), F32),
            v((8, 8, 768), F32),
            v((8, 768), F32),
            v((8, 8, 768), F32),
            dma((10,)),
            dma,
            dma,
            dma((NCH,)),
            dma((NCH,)),
            dma((NCH,)),
            dma((NCH,)),
            dma((NCH,)),
            dma((NCH,)),
            dma((2,)),
            dma,
            dma,
            dma,
        ],
        name="hyena",
        compiler_params=pltpu.CompilerParams(
            collective_id=0, has_side_effects=True, vmem_limit_bytes=62 * 2**20
        ),
    )(
        inputs[0], grad_out[0], w_in,
        filter_real.reshape(4096, 16), filter_imag.reshape(4096, 16),
        *consts,
    )
    return (gated[None], grad)


def solution(mesh):
    placed = (
        P("dp", "ctx", None),
        P("dp", "ctx", None),
        P(),
        P("ctx", None, None),
        P("ctx", None, None),
    )
    return jax.shard_map(
        per_device,
        mesh=mesh,
        in_specs=placed,
        out_specs=(P("dp", "ctx", None), P("dp", None)),
        check_vma=False,
    )
```

```python
import math

import jax
import jax.numpy as jnp
import numpy as np
from jax import lax
from jax.experimental import pallas as pl
from jax.experimental.pallas import tpu as pltpu
from jax.sharding import PartitionSpec as P

N1 = 512
N2 = 512
ROWS = 272
NCH = 2
MESH = pl.DeviceIdType.MESH
BF = jnp.bfloat16
F32 = jnp.float32


def tables():
    half = N1 // 2
    period = N1 * N2
    t1 = np.arange(half)
    fwd = np.zeros((2 * ROWS, half), np.float64)
    inv = np.zeros((half, 2 * ROWS), np.float64)
    base = np.zeros((2, ROWS // 8), np.int64)
    for zh in range(2):
        rows = np.concatenate(
            [zh * half + np.arange(half), (1 - zh) * half + np.arange(8), np.zeros(8, np.int64)]
        )
        base[zh] = rows[::8]
        if zh:
            continue
        angle = 2.0 * np.pi * ((rows[:, None] * t1[None, :]) % N1) / N1
        scale = 1.0 / math.sqrt(N1)
        cos = (np.cos(angle) * scale).astype(BF).astype(np.float64)
        sin = (np.sin(angle) * scale).astype(BF).astype(np.float64)
        cos[half + 8 :] = 0.0
        sin[half + 8 :] = 0.0
        fwd[:ROWS] = cos
        fwd[ROWS:] = -sin
        weight = np.where((rows == 0) | (rows == half), 1.0, 2.0)
        weight[half + 1 :] = 0.0
        inv[:, :ROWS] = (weight[:, None] * cos).T
        inv[:, ROWS:] = -(weight[:, None] * sin).T
    t2 = np.arange(N2)
    angle = 2.0 * np.pi * ((t2[:, None] * t2[None, :]) % N2) / N2
    cos2 = np.cos(angle) / math.sqrt(N2)
    sin2 = np.sin(angle) / math.sqrt(N2)
    two = np.stack([cos2, sin2])
    coarse = 2.0 * np.pi * ((base[:, :, None] * t2) % period) / period
    fine = 2.0 * np.pi * ((np.arange(8)[:, None] * t2) % period) / period
    coarse = np.stack([np.cos(coarse), np.sin(coarse)], axis=1)[:, :, :, None, :]
    fine = np.stack([np.cos(fine), np.sin(fine)])
    order = np.arange(128)
    zh, g, i4 = order // 64, (order // 4) % 16, order % 4
    perm = np.zeros((128, 128))
    perm[order, zh * 64 + i4 * 16 + g] = 1.0
    return (
        fwd.astype(BF),
        inv.astype(BF),
        two.astype(BF),
        coarse.astype(np.float32),
        fine.astype(np.float32),
        perm.astype(BF),
        perm.T.copy().astype(BF),
        np.eye(256).astype(BF),
    )


def nt(a, b):
    return lax.dot_general(a, b, (((1,), (1,)), ((), ())), preferred_element_type=F32)


def nn(a, b):
    return jnp.dot(a, b, preferred_element_type=F32)


def mingle(a, b):
    low = lax.broadcasted_iota(jnp.int32, a.shape, 1) < 4
    first = jnp.where(low, a, pltpu.roll(b, 4, 1))
    second = jnp.where(low, pltpu.roll(a, 4, 1), b)
    return first, second


def kernel(
    x_any, g_any, w_any, fr_any, fi_any, fwd_any, inv_any, two_any, coarse_any, fine_ref,
    perm_ref, permt_ref, eye_ref,
    out_ref, grad_ref,
    x_ref, g_ref, w_ref, fr_in, fi_in, coarse_ref, fwd, inv, tab2, tab3, xt, wt, feat, gt, fsc, fsend, frecv, fre, fim, twc, tws,
    send_in, recv_in, mix, spec, prod, ret, send_out, recv_out,
    part, precv, zsend, zrecv, fin, frows, smoothed,
    tab_sem, fsem_s, fsem_r, in_s, in_r, out_s, out_r, p_s, p_r, z_s, z_r, g_s, g_r,
):
    zl = lax.axis_index("dp")
    ctx = lax.axis_index("ctx")
    core = ctx % 2
    s = ctx % 32
    zh = ctx // 32
    chip = s // 2

    def ctx_peer(o):
        oc, oy, ox, oz = o % 2, (o // 2) % 4, (o // 8) % 4, o // 32
        cy, cx = (ctx // 2) % 4, (ctx // 8) % 4
        return ((((zh + oz) % 2) * 4 + (cx + ox) % 4) * 4 + (cy + oy) % 4) * 2 + (core + oc) % 2

    barrier = pltpu.get_barrier_semaphore()

    def greet(o, carry):
        pl.semaphore_signal(barrier, inc=1, device_id={"ctx": ctx_peer(o)}, device_id_type=MESH)
        return carry

    lax.fori_loop(1, 64, greet, 0)

    def greet_z(o, carry):
        pl.semaphore_signal(
            barrier,
            inc=1,
            device_id={"dp": (zl + 1 + o // 2) % 4, "ctx": (o % 2) * 32 + s},
            device_id_type=MESH,
        )
        return carry

    lax.fori_loop(0, 6, greet_z, 0)

    inputs = [
        pltpu.make_async_copy(w_any, w_ref, tab_sem.at[8]),
        pltpu.make_async_copy(x_any, x_ref, tab_sem.at[9]),
        pltpu.make_async_copy(g_any, g_ref, tab_sem.at[10]),
        pltpu.make_async_copy(fr_any, fr_in, tab_sem.at[11]),
        pltpu.make_async_copy(fi_any, fi_in, tab_sem.at[12]),
        pltpu.make_async_copy(coarse_any.at[zh], coarse_ref, tab_sem.at[13]),
    ]
    for load in inputs:
        load.start()
    loads = [
        pltpu.make_async_copy(fwd_any, fwd, tab_sem.at[0]),
        pltpu.make_async_copy(inv_any, inv, tab_sem.at[1]),
        pltpu.make_async_copy(two_any.at[0], tab2.at[0:512, 0:512], tab_sem.at[2]),
        pltpu.make_async_copy(two_any.at[0], tab2.at[512:1024, 512:1024], tab_sem.at[3]),
        pltpu.make_async_copy(two_any.at[1], tab2.at[512:1024, 0:512], tab_sem.at[4]),
        pltpu.make_async_copy(two_any.at[0], tab3.at[0:512, 0:512], tab_sem.at[5]),
        pltpu.make_async_copy(two_any.at[0], tab3.at[512:1024, 512:1024], tab_sem.at[6]),
        pltpu.make_async_copy(two_any.at[1], tab3.at[0:512, 512:1024], tab_sem.at[7]),
    ]
    for load in loads:
        load.start()

    inputs[0].wait()
    for h in range(NCH):
        for p in range(3):
            cols = w_ref[:, p * 256 + h * 128 : p * 256 + (h + 1) * 128]
            wt[h, p * 128 : (p + 1) * 128, :] = nt(perm_ref[...], cols).astype(BF)

    def project(h):
        for jj in range(2):
            mixed, turned = [], []
            for j in (2 * jj, 2 * jj + 1):
                xs = x_ref[j * 512 : (j + 1) * 512, :]
                rows = nt(wt[h], xs).astype(BF)
                feat[h, j] = rows
                rows = rows.astype(F32)
                mixed.append((rows[128:256] * rows[256:384]).reshape(16, 8, 512))
                gs = nt(perm_ref[...], g_ref[j * 512 : (j + 1) * 512, h * 128 : (h + 1) * 128])
                gt[h, j] = gs.astype(BF)
                turned.append((gs * rows[0:128]).reshape(16, 8, 512))
            for kind, pair in enumerate((mixed, turned)):
                even, odd = mingle(pair[0], pair[1])
                mix[kind, :, 0, jj * 8 : jj * 8 + 8, :] = even
                mix[kind, :, 1, jj * 8 : jj * 8 + 8, :] = odd
        for kind in range(2):
            block = mix[kind].reshape(32, 16, 512).astype(BF)
            send_in[h, :, kind] = block

    def offset(k):
        return (k + 31) % 63 + 1

    def in_copy(h, k):
        peer = ctx_peer(offset(k))
        return pltpu.make_async_remote_copy(
            send_in.at[h, peer // 2, peer % 2],
            recv_in.at[h, ctx],
            in_s.at[h],
            in_r.at[h],
            device_id={"ctx": peer},
            device_id_type=MESH,
        )

    def send_chunk(h):
        def step(k, carry):
            in_copy(h, k).start()
            return carry

        lax.fori_loop(0, 63, step, 0)
        recv_in[h, ctx] = send_in[h, ctx // 2, ctx % 2]

    def filter_copy(o):
        peer = zh * 32 + ctx_peer(o) % 32
        return pltpu.make_async_remote_copy(
            fsend.at[(peer // 2) % 16],
            frecv.at[s],
            fsem_s,
            fsem_r,
            device_id={"ctx": peer},
            device_id_type=MESH,
        )

    def extra_copy(o):
        peer = (1 - zh) * 32 + o
        return pltpu.make_async_remote_copy(
            fsend.at[(peer // 2) % 16],
            frecv.at[32],
            fsem_s,
            fsem_r,
            device_id={"ctx": peer},
            device_id_type=MESH,
        )

    inputs[1].wait()
    inputs[2].wait()
    project(0)
    pl.semaphore_wait(barrier, 69)
    send_chunk(0)

    inputs[3].wait()
    inputs[4].wait()
    for which, ref in enumerate((fr_in, fi_in)):
        for k in range(8):
            turned = ref[k]
            for q in range(4):
                fsc[q, pl.ds(which * 8 + k, 16, stride=16), :] = turned[
                    :, q * 128 : (q + 1) * 128
                ]
    for q in range(4):
        fsend[:, :, q * 128 : (q + 1) * 128] = fsc[q].reshape(16, 16, 128).astype(BF)

    def fstep(o, carry):
        filter_copy(o).start()
        return carry

    lax.fori_loop(1, 32, fstep, 0)
    frecv[s] = fsend[chip]

    @pl.when(s == 0)
    def _():
        def estep(o, carry):
            extra_copy(o).start()
            return carry

        lax.fori_loop(0, 32, estep, 0)

    frecv[33] = jnp.zeros((16, 512), BF)

    project(1)
    send_chunk(1)

    for j in range(4):
        xt[j] = nt(eye_ref[...], x_ref[j * 512 : (j + 1) * 512, :]).astype(BF)
    inputs[5].wait()
    ca, sa = coarse_ref[0], coarse_ref[1]
    cb, sb = fine_ref[0][None], fine_ref[1][None]
    twc[...] = (ca * cb - sa * sb).reshape(ROWS, 512)
    tws[...] = (sa * cb + ca * sb).reshape(ROWS, 512)
    for load in loads:
        load.wait()
    tab2[0:512, 512:1024] = -tab2[512:1024, 0:512]
    tab3[512:1024, 0:512] = -tab3[0:512, 512:1024]
    odd = lax.broadcasted_iota(jnp.int32, (2 * ROWS, 256), 1) % 2
    fwd[...] = jnp.where(odd * zh == 1, -fwd[...].astype(F32), fwd[...].astype(F32)).astype(BF)
    odd = lax.broadcasted_iota(jnp.int32, (256, 2 * ROWS), 0) % 2
    inv[...] = jnp.where(odd * zh == 1, -inv[...].astype(F32), inv[...].astype(F32)).astype(BF)
    pltpu.make_async_copy(frecv.at[pl.ds(0, 32)], frecv.at[pl.ds(0, 32)], fsem_r).wait()
    both = frecv[...].astype(F32)
    sign = (1 - 2 * core).astype(F32)
    fre[...] = both[:, 0:8].reshape(ROWS, 512)
    fim[...] = both[:, 8:16].reshape(ROWS, 512) * sign

    def out_copy(h, k):
        peer = ctx_peer(offset(k))
        return pltpu.make_async_remote_copy(
            send_out.at[h, peer],
            recv_out.at[h, ctx // 4, (ctx // 2) % 2, core],
            out_s.at[h],
            out_r.at[h],
            device_id={"ctx": peer},
            device_id_type=MESH,
        )

    def conv(h, carry):
        pltpu.make_async_copy(
            recv_in.at[h, pl.ds(0, 63)], recv_in.at[h, pl.ds(0, 63)], in_r.at[h]
        ).wait()
        for q in range(4):
            lanes = slice(q * 128, (q + 1) * 128)
            spec[q] = recv_in[h, :, :, lanes].astype(F32).reshape(1024, 128)
        for i in range(4):
            sig = jnp.concatenate(
                [spec[q, pl.ds(i, 256, stride=4), :] for q in range(4)], axis=1
            ).astype(BF)
            one = nn(fwd[...], sig)
            re, im = one[:ROWS], one[ROWS:]
            c, sn = twc[...], tws[...]
            prod[:, 0:512] = (re * c + im * sn).astype(BF)
            prod[:, 512:1024] = (im * c - re * sn).astype(BF)
            two = nn(prod[...], tab2[...])
            dr, di = two[:, 0:512], two[:, 512:1024]
            a, b = fre[...], fim[...]
            prod[:, 0:512] = (dr * a - di * b).astype(BF)
            prod[:, 512:1024] = (dr * b + di * a).astype(BF)
            three = nn(prod[...], tab3[...])
            er, ei = three[:, 0:512], three[:, 512:1024]
            c, sn = twc[...], tws[...]
            ret[0:ROWS, :] = (er * c - ei * sn).astype(BF)
            ret[ROWS:, :] = (ei * c + er * sn).astype(BF)
            four = nn(inv[...], ret[...])
            for q in range(4):
                spec[q, pl.ds(i, 256, stride=4), :] = four[:, q * 128 : (q + 1) * 128]
        for q in range(4):
            lanes = slice(q * 128, (q + 1) * 128)
            send_out[h, :, :, lanes] = spec[q].reshape(64, 16, 128).astype(BF)

        def step(k, inner):
            out_copy(h, k).start()
            return inner

        lax.fori_loop(0, 63, step, 0)
        recv_out[h, ctx // 4, (ctx // 2) % 2, core] = send_out[h, ctx]
        return carry

    lax.fori_loop(0, NCH, conv, 0)

    owner = s % 4
    unit = s // 4
    here = zh * 4 + zl

    def part_copy(h, o):
        peer = ctx_peer(o) % 32
        return pltpu.make_async_remote_copy(
            part.at[h, (peer % 4) * 8 + peer // 4],
            precv.at[h, s],
            p_s.at[h],
            p_r.at[h],
            device_id={"ctx": zh * 32 + peer},
            device_id_type=MESH,
        )

    def grads(h):
        pltpu.make_async_copy(
            send_out.at[h, pl.ds(0, 63)], send_out.at[h, pl.ds(0, 63)], out_r.at[h]
        ).wait()
        total = jnp.zeros((256, 384), F32)
        for jj in range(2):
            got = []
            for kind in range(2):
                even = recv_out[h, :, 0, kind].astype(F32)[:, jj * 8 : jj * 8 + 8]
                odd = recv_out[h, :, 1, kind].astype(F32)[:, jj * 8 : jj * 8 + 8]
                first, second = mingle(even, odd)
                got.append((first.reshape(128, 512), second.reshape(128, 512)))
            for q in range(2):
                j = 2 * jj + q
                smooth, mixed = got[0][q], got[1][q]
                smoothed[j] = smooth.astype(BF)
                rows = feat[h, j, 128:384].astype(F32)
                key, value = rows[0:128], rows[128:256]
                terms = []
                for term in (gt[h, j].astype(F32) * smooth, mixed * value, mixed * key):
                    terms.append(nn(permt_ref[...], term.astype(BF)).astype(BF))
                total = total + nt(xt[j], jnp.concatenate(terms, axis=0))
        part[h] = total.reshape(32, 8, 384)

        def step(o, inner):
            part_copy(h, o).start()
            return inner

        lax.fori_loop(1, 32, step, 0)
        precv[h, s] = part[h, owner * 8 + unit]

    def gates(h):
        for j in range(4):
            gate = feat[h, j, 0:128].astype(F32)
            gated = (gate * smoothed[j].astype(F32)).astype(BF)
            gated = nn(permt_ref[...], gated)
            out_ref[j * 512 : (j + 1) * 512, h * 128 : (h + 1) * 128] = gated.T.astype(BF)

    def z_copy(h, half):
        return pltpu.make_async_remote_copy(
            zsend.at[h],
            zrecv.at[h, here],
            z_s.at[h, half],
            z_r.at[h],
            device_id={"dp": owner, "ctx": half * 32 + s},
            device_id_type=MESH,
        )

    def across(h):
        pltpu.make_async_copy(
            part.at[h, pl.ds(0, 31)], part.at[h, pl.ds(0, 31)], p_r.at[h]
        ).wait()
        zsend[h] = jnp.sum(precv[h], axis=0)
        for half in range(2):
            mine = (zl == owner) & (zh == half)

            @pl.when(mine)
            def _():
                zrecv[h, here] = zsend[h]

            @pl.when(jnp.logical_not(mine))
            def _():
                z_copy(h, half).start()

    def g_copy(h, o):
        return pltpu.make_async_remote_copy(
            fin.at[h],
            frows.at[h, unit],
            g_s.at[h],
            g_r.at[h],
            device_id={"ctx": zh * 32 + ctx_peer(o) % 32},
            device_id_type=MESH,
        )

    def share(h):
        @pl.when(zl == owner)
        def _():
            pltpu.make_async_copy(
                zrecv.at[h, pl.ds(0, 7)], zrecv.at[h, pl.ds(0, 7)], z_r.at[h]
            ).wait()
            fin[h] = jnp.sum(zrecv[h], axis=0) * (1.0 / math.sqrt(524288.0))

            def step(o, inner):
                g_copy(h, o).start()
                return inner

            lax.fori_loop(1, 32, step, 0)
            frows[h, unit] = fin[h]

    grads(0)
    gates(0)
    across(0)
    grads(1)
    share(0)
    gates(1)
    across(1)
    share(1)

    for h in range(NCH):
        @pl.when(zl == owner)
        def _():
            pltpu.make_async_copy(
                frows.at[h, pl.ds(0, 7)], frows.at[h, pl.ds(0, 7)], g_r.at[h]
            ).wait()

        @pl.when(zl != owner)
        def _():
            pltpu.make_async_copy(frows.at[h], frows.at[h], g_r.at[h]).wait()

        done = frows[h].reshape(64, 384)
        for p in range(3):
            grad_ref[:, p * 256 + h * 128 : p * 256 + (h + 1) * 128] = done[
                :, p * 128 : (p + 1) * 128
            ]

    for h in range(NCH):
        for buf, sem in ((recv_in, in_s), (send_out, out_s)):
            pltpu.make_async_copy(
                buf.at[h, pl.ds(0, 63)], buf.at[h, pl.ds(0, 63)], sem.at[h]
            ).wait()
        pltpu.make_async_copy(
            part.at[h, pl.ds(0, 31)], part.at[h, pl.ds(0, 31)], p_s.at[h]
        ).wait()

    pltpu.make_async_copy(frecv.at[pl.ds(0, 31)], frecv.at[pl.ds(0, 31)], fsem_s).wait()

    @pl.when(s == 0)
    def _():
        pltpu.make_async_copy(frecv.at[pl.ds(0, 32)], frecv.at[pl.ds(0, 32)], fsem_s).wait()

    for h in range(NCH):
        for half in range(2):
            @pl.when(jnp.logical_not((zl == owner) & (zh == half)))
            def _():
                z_copy(h, half).wait_send()

        @pl.when(zl == owner)
        def _():
            pltpu.make_async_copy(
                precv.at[h, pl.ds(0, 31)], precv.at[h, pl.ds(0, 31)], g_s.at[h]
            ).wait()


def per_device(inputs, grad_out, w_in, filter_real, filter_imag):
    consts = [jnp.asarray(t) for t in tables()]
    vm = pl.BlockSpec(memory_space=pltpu.VMEM)
    anyspace = pl.BlockSpec(memory_space=pl.ANY)
    v = pltpu.VMEM
    dma = pltpu.SemaphoreType.DMA
    gated, grad = pl.pallas_call(
        kernel,
        out_shape=(
            pltpu.VMEM((2048, 256), BF),
            pltpu.VMEM((64, 768), F32),
        ),
        in_specs=[anyspace] * 9 + [vm] * 4,
        out_specs=(vm, vm),
        scratch_shapes=[
            v((2048, 256), BF),
            v((2048, 256), BF),
            v((256, 768), BF),
            v((8, 16, 512), F32),
            v((8, 16, 512), F32),
            v((2, ROWS // 8, 1, 512), F32),
            v((2 * ROWS, 256), BF),
            v((256, 2 * ROWS), BF),
            v((1024, 1024), BF),
            v((1024, 1024), BF),
            v((4, 256, 512), BF),
            v((NCH, 384, 256), BF),
            v((NCH, 4, 384, 512), BF),
            v((NCH, 4, 128, 512), BF),
            v((4, 256, 128), F32),
            v((16, 16, 512), BF),
            v((34, 16, 512), BF),
            v((ROWS, 512), F32),
            v((ROWS, 512), F32),
            v((ROWS, 512), F32),
            v((ROWS, 512), F32),
            v((NCH, 32, 2, 16, 512), BF),
            v((NCH, 64, 16, 512), BF),
            v((2, 16, 2, 16, 512), F32),
            v((4, 1024, 128), F32),
            v((ROWS, 1024), BF),
            v((2 * ROWS, 512), BF),
            v((NCH, 64, 16, 512), BF),
            v((NCH, 16, 2, 2, 16, 512), BF),
            v((NCH, 32, 8, 384), F32),
            v((NCH, 32, 8, 384), F32),
            v((NCH, 8, 384), F32),
            v((NCH, 8, 8, 384), F32),
            v((NCH, 8, 384), F32),
            v((NCH, 8, 8, 384), F32),
            v((4, 128, 512), BF),
            dma((14,)),
            dma,
            dma,
            dma((NCH,)),
            dma((NCH,)),
            dma((NCH,)),
            dma((NCH,)),
            dma((NCH,)),
            dma((NCH,)),
            dma((NCH, 2)),
            dma((NCH,)),
            dma((NCH,)),
            dma((NCH,)),
        ],
        name="hyena",
        compiler_params=pltpu.CompilerParams(
            collective_id=0, has_side_effects=True, vmem_limit_bytes=62 * 2**20
        ),
    )(
        inputs[0], grad_out[0], w_in,
        jnp.transpose(filter_real, (0, 2, 1)), jnp.transpose(filter_imag, (0, 2, 1)),
        *consts,
    )
    return (gated[None], grad)


def solution(mesh):
    placed = (
        P("dp", "ctx", None),
        P("dp", "ctx", None),
        P(),
        P("ctx", None, None),
        P("ctx", None, None),
    )
    return jax.shard_map(
        per_device,
        mesh=mesh,
        in_specs=placed,
        out_specs=(P("dp", "ctx", None), P("dp", None)),
        check_vma=False,
    )
```

```python
import math

import jax
import jax.numpy as jnp
import numpy as np
from jax import lax
from jax.experimental import pallas as pl
from jax.experimental.pallas import tpu as pltpu
from jax.sharding import PartitionSpec as P

N1 = 512
N2 = 512
ROWS = 272
NCH = 2
MESH = pl.DeviceIdType.MESH
BF = jnp.bfloat16
F32 = jnp.float32


def tables():
    half = N1 // 2
    period = N1 * N2
    t1 = np.arange(half)
    fwd = np.zeros((2 * ROWS, half), np.float64)
    inv = np.zeros((half, 2 * ROWS), np.float64)
    base = np.zeros((2, ROWS // 8), np.int64)
    for zh in range(2):
        rows = np.concatenate(
            [zh * half + np.arange(half), (1 - zh) * half + np.arange(8), np.zeros(8, np.int64)]
        )
        base[zh] = rows[::8]
        if zh:
            continue
        angle = 2.0 * np.pi * ((rows[:, None] * t1[None, :]) % N1) / N1
        scale = 1.0 / math.sqrt(N1)
        cos = (np.cos(angle) * scale).astype(BF).astype(np.float64)
        sin = (np.sin(angle) * scale).astype(BF).astype(np.float64)
        cos[half + 8 :] = 0.0
        sin[half + 8 :] = 0.0
        fwd[:ROWS] = cos
        fwd[ROWS:] = -sin
        weight = np.where((rows == 0) | (rows == half), 1.0, 2.0)
        weight[half + 1 :] = 0.0
        inv[:, :ROWS] = (weight[:, None] * cos).T
        inv[:, ROWS:] = -(weight[:, None] * sin).T
    t2 = np.arange(N2)
    angle = 2.0 * np.pi * ((t2[:, None] * t2[None, :]) % N2) / N2
    cos2 = np.cos(angle) / math.sqrt(N2)
    sin2 = np.sin(angle) / math.sqrt(N2)
    two = np.stack([cos2, sin2])
    coarse = 2.0 * np.pi * ((base[:, :, None] * t2) % period) / period
    fine = 2.0 * np.pi * ((np.arange(8)[:, None] * t2) % period) / period
    coarse = np.stack([np.cos(coarse), np.sin(coarse)], axis=1)[:, :, :, None, :]
    fine = np.stack([np.cos(fine), np.sin(fine)])
    order = np.arange(128)
    zh, g, i4 = order // 64, (order // 4) % 16, order % 4
    perm = np.zeros((128, 128))
    perm[order, zh * 64 + i4 * 16 + g] = 1.0
    return (
        fwd.astype(BF),
        inv.astype(BF),
        two.astype(BF),
        coarse.astype(np.float32),
        fine.astype(np.float32),
        perm.astype(BF),
        perm.T.copy().astype(BF),
        np.eye(256).astype(BF),
    )


def nt(a, b):
    return lax.dot_general(a, b, (((1,), (1,)), ((), ())), preferred_element_type=F32)


def nn(a, b):
    return jnp.dot(a, b, preferred_element_type=F32)


def mingle(a, b):
    low = lax.broadcasted_iota(jnp.int32, a.shape, 1) < 4
    first = jnp.where(low, a, pltpu.roll(b, 4, 1))
    second = jnp.where(low, pltpu.roll(a, 4, 1), b)
    return first, second


def kernel(
    x_any, g_any, w_any, fr_any, fi_any, fwd_any, inv_any, two_any, coarse_any, fine_ref,
    perm_ref, permt_ref, eye_ref,
    out_ref, grad_ref,
    x_ref, g_ref, w_ref, fr_in, fi_in, coarse_ref, fwd, inv, tab2, tab3, xt, wt, feat, gt, fsc, fsend, frecv, fre, fim, twc, tws,
    send_in, recv_in, mix, spec, prod, ret, send_out, recv_out,
    part, precv, zsend, zrecv, fin, frows, smoothed,
    tab_sem, fsem_s, fsem_r, in_s, in_r, out_s, out_r, p_s, p_r, z_s, z_r, g_s, g_r,
):
    zl = lax.axis_index("dp")
    ctx = lax.axis_index("ctx")
    core = ctx % 2
    s = ctx % 32
    zh = ctx // 32
    chip = s // 2

    def ctx_peer(o):
        oc, oy, ox, oz = o % 2, (o // 2) % 4, (o // 8) % 4, o // 32
        cy, cx = (ctx // 2) % 4, (ctx // 8) % 4
        return ((((zh + oz) % 2) * 4 + (cx + ox) % 4) * 4 + (cy + oy) % 4) * 2 + (core + oc) % 2

    barrier = pltpu.get_barrier_semaphore()

    def greet(o, carry):
        pl.semaphore_signal(barrier, inc=1, device_id={"ctx": ctx_peer(o)}, device_id_type=MESH)
        return carry

    lax.fori_loop(1, 64, greet, 0)

    def greet_z(o, carry):
        pl.semaphore_signal(
            barrier,
            inc=1,
            device_id={"dp": (zl + 1 + o // 2) % 4, "ctx": (o % 2) * 32 + s},
            device_id_type=MESH,
        )
        return carry

    lax.fori_loop(0, 6, greet_z, 0)

    inputs = [
        pltpu.make_async_copy(w_any, w_ref, tab_sem.at[8]),
        pltpu.make_async_copy(x_any, x_ref, tab_sem.at[9]),
        pltpu.make_async_copy(g_any, g_ref, tab_sem.at[10]),
        pltpu.make_async_copy(fr_any, fr_in, tab_sem.at[11]),
        pltpu.make_async_copy(fi_any, fi_in, tab_sem.at[12]),
        pltpu.make_async_copy(coarse_any.at[zh], coarse_ref, tab_sem.at[13]),
    ]
    for load in inputs:
        load.start()
    loads = [
        pltpu.make_async_copy(fwd_any, fwd, tab_sem.at[0]),
        pltpu.make_async_copy(inv_any, inv, tab_sem.at[1]),
        pltpu.make_async_copy(two_any.at[0], tab2.at[0:512, 0:512], tab_sem.at[2]),
        pltpu.make_async_copy(two_any.at[0], tab2.at[512:1024, 512:1024], tab_sem.at[3]),
        pltpu.make_async_copy(two_any.at[1], tab2.at[512:1024, 0:512], tab_sem.at[4]),
        pltpu.make_async_copy(two_any.at[0], tab3.at[0:512, 0:512], tab_sem.at[5]),
        pltpu.make_async_copy(two_any.at[0], tab3.at[512:1024, 512:1024], tab_sem.at[6]),
        pltpu.make_async_copy(two_any.at[1], tab3.at[0:512, 512:1024], tab_sem.at[7]),
    ]
    for load in loads:
        load.start()

    inputs[0].wait()
    for h in range(NCH):
        for p in range(3):
            cols = w_ref[:, p * 256 + h * 128 : p * 256 + (h + 1) * 128]
            wt[h, p * 128 : (p + 1) * 128, :] = nt(perm_ref[...], cols).astype(BF)

    def project(h):
        for jj in range(2):
            mixed, turned = [], []
            for j in (2 * jj, 2 * jj + 1):
                xs = x_ref[j * 512 : (j + 1) * 512, :]
                rows = nt(wt[h], xs).astype(BF)
                feat[h, j] = rows
                rows = rows.astype(F32)
                mixed.append((rows[128:256] * rows[256:384]).reshape(16, 8, 512))
                gs = nt(perm_ref[...], g_ref[j * 512 : (j + 1) * 512, h * 128 : (h + 1) * 128])
                gt[h, j] = gs.astype(BF)
                turned.append((gs * rows[0:128]).reshape(16, 8, 512))
            for kind, pair in enumerate((mixed, turned)):
                even, odd = mingle(pair[0], pair[1])
                mix[kind, :, 0, jj * 8 : jj * 8 + 8, :] = even
                mix[kind, :, 1, jj * 8 : jj * 8 + 8, :] = odd
        for kind in range(2):
            block = mix[kind].reshape(32, 16, 512).astype(BF)
            send_in[h, :, kind] = block

    def offset(k):
        return (k + 31) % 63 + 1

    def in_copy(h, k):
        peer = ctx_peer(offset(k))
        return pltpu.make_async_remote_copy(
            send_in.at[h, peer // 2, peer % 2],
            recv_in.at[h, ctx],
            in_s.at[h],
            in_r.at[h],
            device_id={"ctx": peer},
            device_id_type=MESH,
        )

    def send_chunk(h):
        def step(k, carry):
            in_copy(h, k).start()
            return carry

        lax.fori_loop(0, 63, step, 0)
        recv_in[h, ctx] = send_in[h, ctx // 2, ctx % 2]

    def filter_copy(o):
        peer = zh * 32 + ctx_peer(o) % 32
        return pltpu.make_async_remote_copy(
            fsend.at[(peer // 2) % 16],
            frecv.at[s],
            fsem_s,
            fsem_r,
            device_id={"ctx": peer},
            device_id_type=MESH,
        )

    def extra_copy(o):
        peer = (1 - zh) * 32 + o
        return pltpu.make_async_remote_copy(
            fsend.at[(peer // 2) % 16],
            frecv.at[32],
            fsem_s,
            fsem_r,
            device_id={"ctx": peer},
            device_id_type=MESH,
        )

    inputs[1].wait()
    inputs[2].wait()
    project(0)
    pl.semaphore_wait(barrier, 69)
    send_chunk(0)

    inputs[3].wait()
    inputs[4].wait()
    for which, ref in enumerate((fr_in, fi_in)):
        for k in range(8):
            turned = ref[k]
            for q in range(4):
                fsc[q, pl.ds(which * 8 + k, 16, stride=16), :] = turned[
                    :, q * 128 : (q + 1) * 128
                ]
    for q in range(4):
        fsend[:, :, q * 128 : (q + 1) * 128] = fsc[q].reshape(16, 16, 128).astype(BF)

    def fstep(o, carry):
        filter_copy(o).start()
        return carry

    lax.fori_loop(1, 32, fstep, 0)
    frecv[s] = fsend[chip]

    @pl.when(s == 0)
    def _():
        def estep(o, carry):
            extra_copy(o).start()
            return carry

        lax.fori_loop(0, 32, estep, 0)

    frecv[33] = jnp.zeros((16, 512), BF)

    project(1)
    send_chunk(1)

    for j in range(4):
        xt[j] = nt(eye_ref[...], x_ref[j * 512 : (j + 1) * 512, :]).astype(BF)
    inputs[5].wait()
    ca, sa = coarse_ref[0], coarse_ref[1]
    cb, sb = fine_ref[0][None], fine_ref[1][None]
    twc[...] = (ca * cb - sa * sb).reshape(ROWS, 512)
    tws[...] = (sa * cb + ca * sb).reshape(ROWS, 512)
    for load in loads:
        load.wait()
    tab2[0:512, 512:1024] = -tab2[512:1024, 0:512]
    tab3[512:1024, 0:512] = -tab3[0:512, 512:1024]
    odd = lax.broadcasted_iota(jnp.int32, (2 * ROWS, 256), 1) % 2
    fwd[...] = jnp.where(odd * zh == 1, -fwd[...].astype(F32), fwd[...].astype(F32)).astype(BF)
    odd = lax.broadcasted_iota(jnp.int32, (256, 2 * ROWS), 0) % 2
    inv[...] = jnp.where(odd * zh == 1, -inv[...].astype(F32), inv[...].astype(F32)).astype(BF)
    pltpu.make_async_copy(frecv.at[pl.ds(0, 32)], frecv.at[pl.ds(0, 32)], fsem_r).wait()
    both = frecv[...].astype(F32)
    sign = (1 - 2 * core).astype(F32)
    fre[...] = both[:, 0:8].reshape(ROWS, 512)
    fim[...] = both[:, 8:16].reshape(ROWS, 512) * sign

    def out_copy(h, k):
        peer = ctx_peer(offset(k))
        return pltpu.make_async_remote_copy(
            send_out.at[h, peer],
            recv_out.at[h, ctx // 4, (ctx // 2) % 2, core],
            out_s.at[h],
            out_r.at[h, offset(k) // 32],
            device_id={"ctx": peer},
            device_id_type=MESH,
        )

    def conv(h, carry):
        pltpu.make_async_copy(
            recv_in.at[h, pl.ds(0, 63)], recv_in.at[h, pl.ds(0, 63)], in_r.at[h]
        ).wait()
        for q in range(4):
            lanes = slice(q * 128, (q + 1) * 128)
            spec[q] = recv_in[h, :, :, lanes].astype(F32).reshape(1024, 128)
        for i in range(4):
            sig = jnp.concatenate(
                [spec[q, pl.ds(i, 256, stride=4), :] for q in range(4)], axis=1
            ).astype(BF)
            one = nn(fwd[...], sig)
            re, im = one[:ROWS], one[ROWS:]
            c, sn = twc[...], tws[...]
            prod[:, 0:512] = (re * c + im * sn).astype(BF)
            prod[:, 512:1024] = (im * c - re * sn).astype(BF)
            two = nn(prod[...], tab2[...])
            dr, di = two[:, 0:512], two[:, 512:1024]
            a, b = fre[...], fim[...]
            prod[:, 0:512] = (dr * a - di * b).astype(BF)
            prod[:, 512:1024] = (dr * b + di * a).astype(BF)
            three = nn(prod[...], tab3[...])
            er, ei = three[:, 0:512], three[:, 512:1024]
            c, sn = twc[...], tws[...]
            ret[0:ROWS, :] = (er * c - ei * sn).astype(BF)
            ret[ROWS:, :] = (ei * c + er * sn).astype(BF)
            four = nn(inv[...], ret[...])
            for q in range(4):
                spec[q, pl.ds(i, 256, stride=4), :] = four[:, q * 128 : (q + 1) * 128]
        for q in range(4):
            lanes = slice(q * 128, (q + 1) * 128)
            send_out[h, :, :, lanes] = spec[q].reshape(64, 16, 128).astype(BF)

        def step(k, inner):
            out_copy(h, k).start()
            return inner

        lax.fori_loop(0, 63, step, 0)
        recv_out[h, ctx // 4, (ctx // 2) % 2, core] = send_out[h, ctx]
        return carry

    lax.fori_loop(0, NCH, conv, 0)

    owner = s % 4
    unit = s // 4
    here = zh * 4 + zl

    def part_copy(h, half, o):
        peer = ctx_peer(o) % 32
        return pltpu.make_async_remote_copy(
            part.at[h, half, (peer % 4) * 8 + peer // 4],
            precv.at[h, half, s],
            p_s.at[h, half],
            p_r.at[h, half],
            device_id={"ctx": zh * 32 + peer},
            device_id_type=MESH,
        )

    def grads(h, cross):
        count = 31 + cross
        pltpu.make_async_copy(
            send_out.at[h, pl.ds(0, count)], send_out.at[h, pl.ds(0, count)], out_r.at[h, cross]
        ).wait()
        half = (zh + cross) % 2
        eight = pl.ds(pl.multiple_of(half * 8, 8), 8)
        here64 = pl.ds(pl.multiple_of(half * 64, 64), 64)
        keys = pl.ds(pl.multiple_of(128 + half * 64, 64), 64)
        values = pl.ds(pl.multiple_of(256 + half * 64, 64), 64)
        back = permt_ref[0:64, 0:64]
        total = jnp.zeros((256, 192), F32)
        for jj in range(2):
            got = []
            for kind in range(2):
                even = recv_out[h, eight, 0, kind].astype(F32)[:, jj * 8 : jj * 8 + 8]
                odd = recv_out[h, eight, 1, kind].astype(F32)[:, jj * 8 : jj * 8 + 8]
                first, second = mingle(even, odd)
                got.append((first.reshape(64, 512), second.reshape(64, 512)))
            for q in range(2):
                j = 2 * jj + q
                smooth, mixed = got[0][q], got[1][q]
                smoothed[j, here64] = smooth.astype(BF)
                key = feat[h, j, keys].astype(F32)
                value = feat[h, j, values].astype(F32)
                terms = []
                for term in (gt[h, j, here64].astype(F32) * smooth, mixed * value, mixed * key):
                    terms.append(nn(back, term.astype(BF)).astype(BF))
                total = total + nt(xt[j], jnp.concatenate(terms, axis=0))
        part[h, half] = total.reshape(32, 8, 192).astype(BF)

        def step(o, inner):
            part_copy(h, half, o).start()
            return inner

        lax.fori_loop(1, 32, step, 0)
        precv[h, half, s] = part[h, half, owner * 8 + unit]

    def gates(h):
        for j in range(4):
            gate = feat[h, j, 0:128].astype(F32)
            gated = (gate * smoothed[j].astype(F32)).astype(BF)
            gated = nn(permt_ref[...], gated)
            out_ref[j * 512 : (j + 1) * 512, h * 128 : (h + 1) * 128] = gated.T.astype(BF)

    def z_copy(h, half):
        return pltpu.make_async_remote_copy(
            zsend.at[h],
            zrecv.at[h, here],
            z_s.at[h, half],
            z_r.at[h],
            device_id={"dp": owner, "ctx": half * 32 + s},
            device_id_type=MESH,
        )

    def across(h):
        for half in range(2):
            block = part.at[h, half, pl.ds(0, 31)]
            pltpu.make_async_copy(block, block, p_r.at[h, half]).wait()
            zsend[h, half] = jnp.sum(precv[h, half].astype(F32), axis=0)
        for half in range(2):
            mine = (zl == owner) & (zh == half)

            @pl.when(mine)
            def _():
                zrecv[h, here] = zsend[h]

            @pl.when(jnp.logical_not(mine))
            def _():
                z_copy(h, half).start()

    def g_copy(h, o):
        return pltpu.make_async_remote_copy(
            fin.at[h],
            frows.at[h, unit],
            g_s.at[h],
            g_r.at[h],
            device_id={"ctx": zh * 32 + ctx_peer(o) % 32},
            device_id_type=MESH,
        )

    def share(h):
        @pl.when(zl == owner)
        def _():
            pltpu.make_async_copy(
                zrecv.at[h, pl.ds(0, 7)], zrecv.at[h, pl.ds(0, 7)], z_r.at[h]
            ).wait()
            fin[h] = jnp.sum(zrecv[h], axis=0) * (1.0 / math.sqrt(524288.0))

            def step(o, inner):
                g_copy(h, o).start()
                return inner

            lax.fori_loop(1, 32, step, 0)
            frows[h, unit] = fin[h]

    grads(0, 0)
    grads(0, 1)
    gates(0)
    across(0)
    grads(1, 0)
    grads(1, 1)
    share(0)
    gates(1)
    across(1)
    share(1)

    for h in range(NCH):
        @pl.when(zl == owner)
        def _():
            pltpu.make_async_copy(
                frows.at[h, pl.ds(0, 7)], frows.at[h, pl.ds(0, 7)], g_r.at[h]
            ).wait()

        @pl.when(zl != owner)
        def _():
            pltpu.make_async_copy(frows.at[h], frows.at[h], g_r.at[h]).wait()

        for p in range(3):
            grad_ref[:, p * 256 + h * 128 : p * 256 + (h + 1) * 128] = jnp.concatenate(
                [
                    frows[h, :, half].reshape(64, 192)[:, p * 64 : (p + 1) * 64]
                    for half in range(2)
                ],
                axis=1,
            )

    for h in range(NCH):
        for buf, sem in ((recv_in, in_s), (send_out, out_s)):
            pltpu.make_async_copy(
                buf.at[h, pl.ds(0, 63)], buf.at[h, pl.ds(0, 63)], sem.at[h]
            ).wait()
        for half in range(2):
            block = part.at[h, half, pl.ds(0, 31)]
            pltpu.make_async_copy(block, block, p_s.at[h, half]).wait()

    pltpu.make_async_copy(frecv.at[pl.ds(0, 31)], frecv.at[pl.ds(0, 31)], fsem_s).wait()

    @pl.when(s == 0)
    def _():
        pltpu.make_async_copy(frecv.at[pl.ds(0, 32)], frecv.at[pl.ds(0, 32)], fsem_s).wait()

    for h in range(NCH):
        for half in range(2):
            @pl.when(jnp.logical_not((zl == owner) & (zh == half)))
            def _():
                z_copy(h, half).wait_send()

        @pl.when(zl == owner)
        def _():
            for _ in range(31):
                pltpu.make_async_copy(fin.at[h], fin.at[h], g_s.at[h]).wait()


def per_device(inputs, grad_out, w_in, filter_real, filter_imag):
    consts = [jnp.asarray(t) for t in tables()]
    vm = pl.BlockSpec(memory_space=pltpu.VMEM)
    anyspace = pl.BlockSpec(memory_space=pl.ANY)
    v = pltpu.VMEM
    dma = pltpu.SemaphoreType.DMA
    gated, grad = pl.pallas_call(
        kernel,
        out_shape=(
            pltpu.VMEM((2048, 256), BF),
            pltpu.VMEM((64, 768), F32),
        ),
        in_specs=[anyspace] * 9 + [vm] * 4,
        out_specs=(vm, vm),
        scratch_shapes=[
            v((2048, 256), BF),
            v((2048, 256), BF),
            v((256, 768), BF),
            v((8, 16, 512), F32),
            v((8, 16, 512), F32),
            v((2, ROWS // 8, 1, 512), F32),
            v((2 * ROWS, 256), BF),
            v((256, 2 * ROWS), BF),
            v((1024, 1024), BF),
            v((1024, 1024), BF),
            v((4, 256, 512), BF),
            v((NCH, 384, 256), BF),
            v((NCH, 4, 384, 512), BF),
            v((NCH, 4, 128, 512), BF),
            v((4, 256, 128), F32),
            v((16, 16, 512), BF),
            v((34, 16, 512), BF),
            v((ROWS, 512), F32),
            v((ROWS, 512), F32),
            v((ROWS, 512), F32),
            v((ROWS, 512), F32),
            v((NCH, 32, 2, 16, 512), BF),
            v((NCH, 64, 16, 512), BF),
            v((2, 16, 2, 16, 512), F32),
            v((4, 1024, 128), F32),
            v((ROWS, 1024), BF),
            v((2 * ROWS, 512), BF),
            v((NCH, 64, 16, 512), BF),
            v((NCH, 16, 2, 2, 16, 512), BF),
            v((NCH, 2, 32, 8, 192), BF),
            v((NCH, 2, 32, 8, 192), BF),
            v((NCH, 2, 8, 192), F32),
            v((NCH, 8, 2, 8, 192), F32),
            v((NCH, 2, 8, 192), F32),
            v((NCH, 8, 2, 8, 192), F32),
            v((4, 128, 512), BF),
            dma((14,)),
            dma,
            dma,
            dma((NCH,)),
            dma((NCH,)),
            dma((NCH,)),
            dma((NCH, 2)),
            dma((NCH, 2)),
            dma((NCH, 2)),
            dma((NCH, 2)),
            dma((NCH,)),
            dma((NCH,)),
            dma((NCH,)),
        ],
        name="hyena",
        compiler_params=pltpu.CompilerParams(
            collective_id=0, has_side_effects=True, vmem_limit_bytes=62 * 2**20
        ),
    )(
        inputs[0], grad_out[0], w_in,
        jnp.transpose(filter_real, (0, 2, 1)), jnp.transpose(filter_imag, (0, 2, 1)),
        *consts,
    )
    return (gated[None], grad)


def solution(mesh):
    placed = (
        P("dp", "ctx", None),
        P("dp", "ctx", None),
        P(),
        P("ctx", None, None),
        P("ctx", None, None),
    )
    return jax.shard_map(
        per_device,
        mesh=mesh,
        in_specs=placed,
        out_specs=(P("dp", "ctx", None), P("dp", None)),
        check_vma=False,
    )
```

```python
import math

import jax
import jax.numpy as jnp
import numpy as np
from jax import lax
from jax.experimental import pallas as pl
from jax.experimental.pallas import tpu as pltpu
from jax.sharding import PartitionSpec as P

N1 = 512
N2 = 512
ROWS = 272
NCH = 2
MESH = pl.DeviceIdType.MESH
BF = jnp.bfloat16
F32 = jnp.float32


def tables():
    half = N1 // 2
    period = N1 * N2
    t1 = np.arange(half)
    fwd = np.zeros((2 * ROWS, half), np.float64)
    inv = np.zeros((half, 2 * ROWS), np.float64)
    base = np.zeros((2, ROWS // 8), np.int64)
    for zh in range(2):
        rows = np.concatenate(
            [zh * half + np.arange(half), (1 - zh) * half + np.arange(8), np.zeros(8, np.int64)]
        )
        base[zh] = rows[::8]
        if zh:
            continue
        angle = 2.0 * np.pi * ((rows[:, None] * t1[None, :]) % N1) / N1
        scale = 1.0 / math.sqrt(N1)
        cos = (np.cos(angle) * scale).astype(BF).astype(np.float64)
        sin = (np.sin(angle) * scale).astype(BF).astype(np.float64)
        cos[half + 8 :] = 0.0
        sin[half + 8 :] = 0.0
        fwd[:ROWS] = cos
        fwd[ROWS:] = -sin
        weight = np.where((rows == 0) | (rows == half), 1.0, 2.0)
        weight[half + 1 :] = 0.0
        inv[:, :ROWS] = (weight[:, None] * cos).T
        inv[:, ROWS:] = -(weight[:, None] * sin).T
    t2 = np.arange(N2)
    angle = 2.0 * np.pi * ((t2[:, None] * t2[None, :]) % N2) / N2
    cos2 = np.cos(angle) / math.sqrt(N2)
    sin2 = np.sin(angle) / math.sqrt(N2)
    two = np.stack([cos2, sin2])
    coarse = 2.0 * np.pi * ((base[:, :, None] * t2) % period) / period
    fine = 2.0 * np.pi * ((np.arange(8)[:, None] * t2) % period) / period
    coarse = np.stack([np.cos(coarse), np.sin(coarse)], axis=1)[:, :, :, None, :]
    fine = np.stack([np.cos(fine), np.sin(fine)])
    order = np.arange(128)
    zh, g, i4 = order // 64, (order // 4) % 16, order % 4
    perm = np.zeros((128, 128))
    perm[order, zh * 64 + i4 * 16 + g] = 1.0
    return (
        fwd.astype(BF),
        inv.astype(BF),
        two.astype(BF),
        coarse.astype(np.float32),
        fine.astype(np.float32),
        perm.astype(BF),
        perm.T.copy().astype(BF),
        np.eye(256).astype(BF),
    )


def nt(a, b):
    return lax.dot_general(a, b, (((1,), (1,)), ((), ())), preferred_element_type=F32)


def nn(a, b):
    return jnp.dot(a, b, preferred_element_type=F32)


def mingle(a, b):
    low = lax.broadcasted_iota(jnp.int32, a.shape, 1) < 4
    first = jnp.where(low, a, pltpu.roll(b, 4, 1))
    second = jnp.where(low, pltpu.roll(a, 4, 1), b)
    return first, second


def kernel(
    x_any, g_any, w_any, fr_any, fi_any, fwd_any, inv_any, two_any, coarse_any, fine_ref,
    perm_ref, permt_ref, eye_ref,
    out_ref, grad_ref,
    x_ref, g_ref, w_ref, fr_in, fi_in, coarse_ref, fwd, inv, tab2, tab3, xt, wt, feat, gt, fsc, fsend, frecv, esc, esend, erecv, fre, fim, twc, tws,
    send_in, recv_in, mix, spec, prod, ret, send_out, recv_out,
    part, precv, zsend, zrecv, fin, frows, smoothed,
    tab_sem, e_s, e_r, fsem_s, fsem_r, in_s, in_r, out_s, out_r, p_s, p_r, z_s, z_r, g_s, g_r,
):
    zl = lax.axis_index("dp")
    ctx = lax.axis_index("ctx")
    core = ctx % 2
    s = ctx % 32
    zh = ctx // 32
    chip = s // 2

    def ctx_peer(o):
        oc, oy, ox, oz = o % 2, (o // 2) % 4, (o // 8) % 4, o // 32
        cy, cx = (ctx // 2) % 4, (ctx // 8) % 4
        return ((((zh + oz) % 2) * 4 + (cx + ox) % 4) * 4 + (cy + oy) % 4) * 2 + (core + oc) % 2

    barrier = pltpu.get_barrier_semaphore()

    def greet(o, carry):
        pl.semaphore_signal(barrier, inc=1, device_id={"ctx": ctx_peer(o)}, device_id_type=MESH)
        return carry

    lax.fori_loop(1, 64, greet, 0)

    def greet_z(o, carry):
        pl.semaphore_signal(
            barrier,
            inc=1,
            device_id={"dp": (zl + 1 + o // 2) % 4, "ctx": (o % 2) * 32 + s},
            device_id_type=MESH,
        )
        return carry

    lax.fori_loop(0, 6, greet_z, 0)

    inputs = [
        pltpu.make_async_copy(w_any, w_ref, tab_sem.at[8]),
        pltpu.make_async_copy(x_any, x_ref, tab_sem.at[9]),
        pltpu.make_async_copy(g_any, g_ref, tab_sem.at[10]),
        pltpu.make_async_copy(fr_any, fr_in, tab_sem.at[11]),
        pltpu.make_async_copy(fi_any, fi_in, tab_sem.at[12]),
        pltpu.make_async_copy(coarse_any.at[zh], coarse_ref, tab_sem.at[13]),
    ]
    for load in inputs:
        load.start()
    loads = [
        pltpu.make_async_copy(fwd_any, fwd, tab_sem.at[0]),
        pltpu.make_async_copy(inv_any, inv, tab_sem.at[1]),
        pltpu.make_async_copy(two_any.at[0], tab2.at[0:512, 0:512], tab_sem.at[2]),
        pltpu.make_async_copy(two_any.at[0], tab2.at[512:1024, 512:1024], tab_sem.at[3]),
        pltpu.make_async_copy(two_any.at[1], tab2.at[512:1024, 0:512], tab_sem.at[4]),
        pltpu.make_async_copy(two_any.at[0], tab3.at[0:512, 0:512], tab_sem.at[5]),
        pltpu.make_async_copy(two_any.at[0], tab3.at[512:1024, 512:1024], tab_sem.at[6]),
        pltpu.make_async_copy(two_any.at[1], tab3.at[0:512, 512:1024], tab_sem.at[7]),
    ]
    for load in loads:
        load.start()

    inputs[0].wait()
    for h in range(NCH):
        for p in range(3):
            cols = w_ref[:, p * 256 + h * 128 : p * 256 + (h + 1) * 128]
            wt[h, p * 128 : (p + 1) * 128, :] = nt(perm_ref[...], cols).astype(BF)

    def project(h):
        for jj in range(2):
            mixed, turned = [], []
            for j in (2 * jj, 2 * jj + 1):
                xs = x_ref[j * 512 : (j + 1) * 512, :]
                rows = nt(wt[h], xs).astype(BF)
                feat[h, j] = rows
                rows = rows.astype(F32)
                mixed.append((rows[128:256] * rows[256:384]).reshape(16, 8, 512))
                gs = nt(perm_ref[...], g_ref[j * 512 : (j + 1) * 512, h * 128 : (h + 1) * 128])
                gt[h, j] = gs.astype(BF)
                turned.append((gs * rows[0:128]).reshape(16, 8, 512))
            for kind, pair in enumerate((mixed, turned)):
                even, odd = mingle(pair[0], pair[1])
                mix[kind, :, 0, jj * 8 : jj * 8 + 8, :] = even
                mix[kind, :, 1, jj * 8 : jj * 8 + 8, :] = odd
        for kind in range(2):
            block = mix[kind].reshape(32, 16, 512).astype(BF)
            send_in[h, :, kind] = block

    def offset(k):
        return (k + 31) % 63 + 1

    def in_copy(h, k):
        peer = ctx_peer(offset(k))
        return pltpu.make_async_remote_copy(
            send_in.at[h, peer // 2, peer % 2],
            recv_in.at[h, ctx],
            in_s.at[h],
            in_r.at[h],
            device_id={"ctx": peer},
            device_id_type=MESH,
        )

    def send_chunk(h):
        def step(k, carry):
            in_copy(h, k).start()
            return carry

        lax.fori_loop(0, 63, step, 0)
        recv_in[h, ctx] = send_in[h, ctx // 2, ctx % 2]

    def filter_copy(o):
        peer = zh * 32 + ctx_peer(o) % 32
        return pltpu.make_async_remote_copy(
            fsend.at[(peer // 2) % 16],
            frecv.at[s],
            fsem_s,
            fsem_r,
            device_id={"ctx": peer},
            device_id_type=MESH,
        )

    def extra_copy(o):
        peer = (1 - zh) * 32 + o
        return pltpu.make_async_remote_copy(
            esend.at[(peer // 2) % 16],
            erecv,
            e_s,
            e_r,
            device_id={"ctx": peer},
            device_id_type=MESH,
        )

    inputs[1].wait()
    inputs[2].wait()
    project(0)
    pl.semaphore_wait(barrier, 69)
    send_chunk(0)

    inputs[3].wait()
    inputs[4].wait()
    for which, ref in enumerate((fr_in, fi_in)):
        for k in range(8):
            turned = ref[k]
            for q in range(4):
                fsc[q, pl.ds(which * 8 + k, 16, stride=16), :] = turned[
                    :, q * 128 : (q + 1) * 128
                ]
    for q in range(4):
        fsend[:, :, q * 128 : (q + 1) * 128] = fsc[q].reshape(16, 16, 128).astype(BF)

    for which, ref in enumerate((fr_in, fi_in)):
        for q in range(4):
            esc[pl.ds(which * 4 + q, 16, stride=8), :] = ref[0][:, q * 128 : (q + 1) * 128]
    esend[...] = esc[...].reshape(16, 8, 128).astype(BF)

    def fstep(o, carry):
        filter_copy(o).start()
        return carry

    lax.fori_loop(1, 32, fstep, 0)
    frecv[s] = fsend[chip]

    @pl.when(s == 0)
    def _():
        def estep(o, carry):
            extra_copy(o).start()
            return carry

        lax.fori_loop(0, 32, estep, 0)


    project(1)
    send_chunk(1)

    for j in range(4):
        xt[j] = nt(eye_ref[...], x_ref[j * 512 : (j + 1) * 512, :]).astype(BF)
    inputs[5].wait()
    ca, sa = coarse_ref[0], coarse_ref[1]
    cb, sb = fine_ref[0][None], fine_ref[1][None]
    twc[...] = (ca * cb - sa * sb).reshape(ROWS, 512)
    tws[...] = (sa * cb + ca * sb).reshape(ROWS, 512)
    for load in loads:
        load.wait()
    tab2[0:512, 512:1024] = -tab2[512:1024, 0:512]
    tab3[512:1024, 0:512] = -tab3[0:512, 512:1024]
    odd = lax.broadcasted_iota(jnp.int32, (2 * ROWS, 256), 1) % 2
    fwd[...] = jnp.where(odd * zh == 1, -fwd[...].astype(F32), fwd[...].astype(F32)).astype(BF)
    odd = lax.broadcasted_iota(jnp.int32, (256, 2 * ROWS), 0) % 2
    inv[...] = jnp.where(odd * zh == 1, -inv[...].astype(F32), inv[...].astype(F32)).astype(BF)
    pltpu.make_async_copy(frecv.at[pl.ds(0, 31)], frecv.at[pl.ds(0, 31)], fsem_r).wait()
    pltpu.make_async_copy(erecv, erecv, e_r).wait()
    both = frecv[...].astype(F32)
    sign = (1 - 2 * core).astype(F32)
    fre[0:256] = both[:, 0:8].reshape(256, 512)
    fim[0:256] = both[:, 8:16].reshape(256, 512) * sign
    more = erecv[...].astype(F32)
    for q in range(4):
        lanes = slice(q * 128, (q + 1) * 128)
        fre[256:264, lanes] = jnp.broadcast_to(more[q : q + 1], (8, 128))
        fim[256:264, lanes] = jnp.broadcast_to(more[q + 4 : q + 5], (8, 128)) * sign
    fre[264:ROWS] = jnp.zeros((8, 512), F32)
    fim[264:ROWS] = jnp.zeros((8, 512), F32)

    def out_copy(h, k):
        peer = ctx_peer(offset(k))
        return pltpu.make_async_remote_copy(
            send_out.at[h, peer],
            recv_out.at[h, ctx // 4, (ctx // 2) % 2, core],
            out_s.at[h],
            out_r.at[h, offset(k) // 32],
            device_id={"ctx": peer},
            device_id_type=MESH,
        )

    def conv(h, carry):
        pltpu.make_async_copy(
            recv_in.at[h, pl.ds(0, 63)], recv_in.at[h, pl.ds(0, 63)], in_r.at[h]
        ).wait()
        for q in range(4):
            lanes = slice(q * 128, (q + 1) * 128)
            spec[q] = recv_in[h, :, :, lanes].astype(F32).reshape(1024, 128)
        for i in range(4):
            sig = jnp.concatenate(
                [spec[q, pl.ds(i, 256, stride=4), :] for q in range(4)], axis=1
            ).astype(BF)
            one = nn(fwd[...], sig)
            re, im = one[:ROWS], one[ROWS:]
            c, sn = twc[...], tws[...]
            prod[:, 0:512] = (re * c + im * sn).astype(BF)
            prod[:, 512:1024] = (im * c - re * sn).astype(BF)
            two = nn(prod[...], tab2[...])
            dr, di = two[:, 0:512], two[:, 512:1024]
            a, b = fre[...], fim[...]
            prod[:, 0:512] = (dr * a - di * b).astype(BF)
            prod[:, 512:1024] = (dr * b + di * a).astype(BF)
            three = nn(prod[...], tab3[...])
            er, ei = three[:, 0:512], three[:, 512:1024]
            c, sn = twc[...], tws[...]
            ret[0:ROWS, :] = (er * c - ei * sn).astype(BF)
            ret[ROWS:, :] = (ei * c + er * sn).astype(BF)
            four = nn(inv[...], ret[...])
            for q in range(4):
                spec[q, pl.ds(i, 256, stride=4), :] = four[:, q * 128 : (q + 1) * 128]
        for q in range(4):
            lanes = slice(q * 128, (q + 1) * 128)
            send_out[h, :, :, lanes] = spec[q].reshape(64, 16, 128).astype(BF)

        def step(k, inner):
            out_copy(h, k).start()
            return inner

        lax.fori_loop(0, 63, step, 0)
        recv_out[h, ctx // 4, (ctx // 2) % 2, core] = send_out[h, ctx]
        return carry

    lax.fori_loop(0, NCH, conv, 0)

    owner = s % 4
    unit = s // 4
    here = zh * 4 + zl

    def part_copy(h, half, o):
        peer = ctx_peer(o) % 32
        return pltpu.make_async_remote_copy(
            part.at[h, half, (peer % 4) * 8 + peer // 4],
            precv.at[h, half, s],
            p_s.at[h, half],
            p_r.at[h, half],
            device_id={"ctx": zh * 32 + peer},
            device_id_type=MESH,
        )

    def grads(h, cross):
        count = 31 + cross
        pltpu.make_async_copy(
            send_out.at[h, pl.ds(0, count)], send_out.at[h, pl.ds(0, count)], out_r.at[h, cross]
        ).wait()
        half = (zh + cross) % 2
        eight = pl.ds(pl.multiple_of(half * 8, 8), 8)
        here64 = pl.ds(pl.multiple_of(half * 64, 64), 64)
        keys = pl.ds(pl.multiple_of(128 + half * 64, 64), 64)
        values = pl.ds(pl.multiple_of(256 + half * 64, 64), 64)
        back = permt_ref[0:64, 0:64]
        total = jnp.zeros((256, 192), F32)
        for jj in range(2):
            got = []
            for kind in range(2):
                even = recv_out[h, eight, 0, kind].astype(F32)[:, jj * 8 : jj * 8 + 8]
                odd = recv_out[h, eight, 1, kind].astype(F32)[:, jj * 8 : jj * 8 + 8]
                first, second = mingle(even, odd)
                got.append((first.reshape(64, 512), second.reshape(64, 512)))
            for q in range(2):
                j = 2 * jj + q
                smooth, mixed = got[0][q], got[1][q]
                smoothed[j, here64] = smooth.astype(BF)
                key = feat[h, j, keys].astype(F32)
                value = feat[h, j, values].astype(F32)
                terms = []
                for term in (gt[h, j, here64].astype(F32) * smooth, mixed * value, mixed * key):
                    terms.append(nn(back, term.astype(BF)).astype(BF))
                total = total + nt(xt[j], jnp.concatenate(terms, axis=0))
        part[h, half] = total.reshape(32, 8, 192).astype(BF)

        def step(o, inner):
            part_copy(h, half, o).start()
            return inner

        lax.fori_loop(1, 32, step, 0)
        precv[h, half, s] = part[h, half, owner * 8 + unit]

    def gates(h):
        for j in range(4):
            gate = feat[h, j, 0:128].astype(F32)
            gated = (gate * smoothed[j].astype(F32)).astype(BF)
            gated = nn(permt_ref[...], gated)
            out_ref[j * 512 : (j + 1) * 512, h * 128 : (h + 1) * 128] = gated.T.astype(BF)

    def z_copy(h, half):
        return pltpu.make_async_remote_copy(
            zsend.at[h],
            zrecv.at[h, here],
            z_s.at[h, half],
            z_r.at[h],
            device_id={"dp": owner, "ctx": half * 32 + s},
            device_id_type=MESH,
        )

    def across(h):
        for half in range(2):
            block = part.at[h, half, pl.ds(0, 31)]
            pltpu.make_async_copy(block, block, p_r.at[h, half]).wait()
            zsend[h, half] = jnp.sum(precv[h, half].astype(F32), axis=0)
        for half in range(2):
            mine = (zl == owner) & (zh == half)

            @pl.when(mine)
            def _():
                zrecv[h, here] = zsend[h]

            @pl.when(jnp.logical_not(mine))
            def _():
                z_copy(h, half).start()

    def g_copy(h, o):
        return pltpu.make_async_remote_copy(
            fin.at[h],
            frows.at[h, unit],
            g_s.at[h],
            g_r.at[h],
            device_id={"ctx": zh * 32 + ctx_peer(o) % 32},
            device_id_type=MESH,
        )

    def share(h):
        @pl.when(zl == owner)
        def _():
            pltpu.make_async_copy(
                zrecv.at[h, pl.ds(0, 7)], zrecv.at[h, pl.ds(0, 7)], z_r.at[h]
            ).wait()
            fin[h] = jnp.sum(zrecv[h], axis=0) * (1.0 / math.sqrt(524288.0))

            def step(o, inner):
                g_copy(h, o).start()
                return inner

            lax.fori_loop(1, 32, step, 0)
            frows[h, unit] = fin[h]

    grads(0, 0)
    grads(0, 1)
    gates(0)
    across(0)
    grads(1, 0)
    grads(1, 1)
    share(0)
    gates(1)
    across(1)
    share(1)

    for h in range(NCH):
        @pl.when(zl == owner)
        def _():
            pltpu.make_async_copy(
                frows.at[h, pl.ds(0, 7)], frows.at[h, pl.ds(0, 7)], g_r.at[h]
            ).wait()

        @pl.when(zl != owner)
        def _():
            pltpu.make_async_copy(frows.at[h], frows.at[h], g_r.at[h]).wait()

        for p in range(3):
            grad_ref[:, p * 256 + h * 128 : p * 256 + (h + 1) * 128] = jnp.concatenate(
                [
                    frows[h, :, half].reshape(64, 192)[:, p * 64 : (p + 1) * 64]
                    for half in range(2)
                ],
                axis=1,
            )

    for h in range(NCH):
        for buf, sem in ((recv_in, in_s), (send_out, out_s)):
            pltpu.make_async_copy(
                buf.at[h, pl.ds(0, 63)], buf.at[h, pl.ds(0, 63)], sem.at[h]
            ).wait()
        for half in range(2):
            block = part.at[h, half, pl.ds(0, 31)]
            pltpu.make_async_copy(block, block, p_s.at[h, half]).wait()

    pltpu.make_async_copy(frecv.at[pl.ds(0, 31)], frecv.at[pl.ds(0, 31)], fsem_s).wait()

    @pl.when(s == 0)
    def _():
        pltpu.make_async_copy(esend, esend, e_s).wait()
        pltpu.make_async_copy(esend, esend, e_s).wait()

    for h in range(NCH):
        for half in range(2):
            @pl.when(jnp.logical_not((zl == owner) & (zh == half)))
            def _():
                z_copy(h, half).wait_send()

        @pl.when(zl == owner)
        def _():
            for _ in range(31):
                pltpu.make_async_copy(fin.at[h], fin.at[h], g_s.at[h]).wait()


def per_device(inputs, grad_out, w_in, filter_real, filter_imag):
    consts = [jnp.asarray(t) for t in tables()]
    vm = pl.BlockSpec(memory_space=pltpu.VMEM)
    anyspace = pl.BlockSpec(memory_space=pl.ANY)
    v = pltpu.VMEM
    dma = pltpu.SemaphoreType.DMA
    gated, grad = pl.pallas_call(
        kernel,
        out_shape=(
            pltpu.VMEM((2048, 256), BF),
            pltpu.VMEM((64, 768), F32),
        ),
        in_specs=[anyspace] * 9 + [vm] * 4,
        out_specs=(vm, vm),
        scratch_shapes=[
            v((2048, 256), BF),
            v((2048, 256), BF),
            v((256, 768), BF),
            v((8, 16, 512), F32),
            v((8, 16, 512), F32),
            v((2, ROWS // 8, 1, 512), F32),
            v((2 * ROWS, 256), BF),
            v((256, 2 * ROWS), BF),
            v((1024, 1024), BF),
            v((1024, 1024), BF),
            v((4, 256, 512), BF),
            v((NCH, 384, 256), BF),
            v((NCH, 4, 384, 512), BF),
            v((NCH, 4, 128, 512), BF),
            v((4, 256, 128), F32),
            v((16, 16, 512), BF),
            v((32, 16, 512), BF),
            v((128, 128), F32),
            v((16, 8, 128), BF),
            v((8, 128), BF),
            v((ROWS, 512), F32),
            v((ROWS, 512), F32),
            v((ROWS, 512), F32),
            v((ROWS, 512), F32),
            v((NCH, 32, 2, 16, 512), BF),
            v((NCH, 64, 16, 512), BF),
            v((2, 16, 2, 16, 512), F32),
            v((4, 1024, 128), F32),
            v((ROWS, 1024), BF),
            v((2 * ROWS, 512), BF),
            v((NCH, 64, 16, 512), BF),
            v((NCH, 16, 2, 2, 16, 512), BF),
            v((NCH, 2, 32, 8, 192), BF),
            v((NCH, 2, 32, 8, 192), BF),
            v((NCH, 2, 8, 192), F32),
            v((NCH, 8, 2, 8, 192), F32),
            v((NCH, 2, 8, 192), F32),
            v((NCH, 8, 2, 8, 192), F32),
            v((4, 128, 512), BF),
            dma((14,)),
            dma,
            dma,
            dma,
            dma,
            dma((NCH,)),
            dma((NCH,)),
            dma((NCH,)),
            dma((NCH, 2)),
            dma((NCH, 2)),
            dma((NCH, 2)),
            dma((NCH, 2)),
            dma((NCH,)),
            dma((NCH,)),
            dma((NCH,)),
        ],
        name="hyena",
        compiler_params=pltpu.CompilerParams(
            collective_id=0, has_side_effects=True, vmem_limit_bytes=62 * 2**20
        ),
    )(
        inputs[0], grad_out[0], w_in,
        jnp.transpose(filter_real, (0, 2, 1)), jnp.transpose(filter_imag, (0, 2, 1)),
        *consts,
    )
    return (gated[None], grad)


def solution(mesh):
    placed = (
        P("dp", "ctx", None),
        P("dp", "ctx", None),
        P(),
        P("ctx", None, None),
        P("ctx", None, None),
    )
    return jax.shard_map(
        per_device,
        mesh=mesh,
        in_specs=placed,
        out_specs=(P("dp", "ctx", None), P("dp", None)),
        check_vma=False,
    )
```
